512 devices in a mesh: expert: 128 (over y, z, core), dp: 4 (over x).
Axes of the slice: x: 4, y: 4, z: 16, core: 2. Of those that a mesh axis runs over, the one named last changes fastest.
Arguments:
- inputs: bfloat16 [16384, 2048], P('expert', 'dp'), may hold values from -6 to 6
- out_grad: bfloat16 [16384, 2048], P('expert', 'dp'), may hold values from -3 to 3
- gate_weights: float32 [16384, 4], P('expert'), may hold values from 0.05 to 0.6
- routes: int32 [16384, 4], P('expert'), may hold values from 0 to 127, all different within a row; in each aligned block of 128 rows (0 to 127, 128 to 255, ...) at most 8 rows name the same one
- up_weight: bfloat16 [128, 768, 2048], P('expert', 'dp'), may hold values from -0.125 to 0.125
- down_weight: bfloat16 [128, 768, 2048], P('expert', 'dp'), may hold values from -0.21875 to 0.21875
Outputs:
- in_grad: bfloat16 [16384, 2048], P('expert', 'dp')
- grad_up: bfloat16 [128, 768, 2048], P('expert', 'dp')
- grad_down: bfloat16 [128, 768, 2048], P('expert', 'dp')
The draws below stay inside these ranges and needn't reach their ends.
Inputs may be any that keep to these rules, and one draw needn't show every extreme that they name: A token's 4 experts differ. Among the routes of the tokens b * 128 to (b + 1) * 128 - 1, no expert is named more than 8 times, a bound that some expert reaches in some of these blocks.
All inputs are finite; a program needn't handle non-finite values.
Results may differ from the reference program's by a relative error of at most 0.015.
Values may be sent and summed in bfloat16 or wider, within the bound.
No kernel may reach another device: no remote copies, remote signals or barrier semaphores. Data moves between devices by JAX's collectives and lax.ppermute only.
A program may use at most 64 MiB of HBM per device.

```python
import math
import jax
import jax.numpy as jnp
import numpy as np
from jax import lax

D = 2048
H = 768
TOP = 4
TOK_DEV = 128
EXPERTS = 128
CAP = 8
HQ = 192
TOKENS = 16384
N_DP = 4


def steps_of(own_key, shape, cuts, smallest, high):
    gain = 1.0
    for position, shards_of in cuts:
        draws = jax.random.uniform(jax.random.fold_in(jax.random.fold_in(own_key, 6), position), (shards_of,), jnp.float32, smallest / len(cuts), high / len(cuts))
        gain = gain * jnp.repeat(jnp.exp(draws), shape[position] // shards_of).reshape((-1,) + (1,) * (len(shape) - 1 - position))
    return gain


def shared_out(stream_key, own, number, rows, amount, top, most, slope):
    ranking = jax.random.permutation(stream_key, amount)
    crowded, usual = shares(amount, rows * top, most, slope, True), shares(amount, rows * top, most, slope, False)
    places = jnp.arange(amount)

    def named(tallies, offset_by):
        used = int((tallies > 0).sum())
        fixed = max(1, used // 4)
        passed = fixed + (places - fixed + offset_by * (used - fixed)) % max(1, amount - fixed)
        return jnp.zeros((amount,), jnp.int32).at[ranking[jnp.where(places < fixed, places, passed)]].set(jnp.asarray(tallies, jnp.int32))

    tallies = jnp.where(number % 4 == 0, named(crowded, number // 4), named(usual, number - number // 4 - 1))
    mixed = jax.random.permutation(jax.random.fold_in(own, 3), amount)
    giver, sink = mixed[0:amount // 2 * 2:2], mixed[1:amount // 2 * 2:2]
    room = jnp.minimum(tallies[giver] - 1, most - tallies[sink]) // 2
    room = jnp.where((giver == ranking[0]) | (sink == ranking[0]) | (tallies[sink] == 0), 0, jnp.maximum(room, 0))
    passed = jax.random.randint(jax.random.fold_in(own, 4), (amount // 2,), 0, 1 << 20) % (room + 1)
    tallies = tallies.at[giver].add(-passed).at[sink].add(passed)
    items = jnp.searchsorted(jnp.cumsum(tallies), jnp.arange(rows * top), side="right").astype(jnp.int32)
    listing = items.reshape(top, rows).T
    listing = listing[jax.random.permutation(jax.random.fold_in(own, 1), rows)]
    offset_by = jax.random.randint(jax.random.fold_in(own, 2), (rows, 1), 0, top)
    return jnp.take_along_axis(listing, (jnp.arange(top)[None, :] + offset_by) % top, axis=1)


def shares(number_of, total, bound, lean, full):
    weights = [(1 << 20) // math.isqrt(rank ** lean) + 1 for rank in range(1, number_of + 1)]
    largest = bound if full else min(bound, max(-(-total // number_of), total * weights[0] // sum(weights)))
    least = 1 if total - largest >= number_of - 1 else 0
    holding, surplus = [largest] + [least] * (number_of - 1), total - largest - least * (number_of - 1)
    while surplus > 0:
        movable = [i for i in range(1, number_of) if holding[i] < largest] or [i for i in range(1, number_of) if holding[i] < bound]
        mass, left = sum([weights[i] for i in movable]), surplus
        for i in movable:
            addition = min(bound - holding[i], max(1, left * weights[i] // mass), surplus)
            holding[i] = holding[i] + addition
            surplus = surplus - addition
    return np.array(holding)


def centred(key, shape, width, most, shards=(), kind=jnp.bfloat16):
    drawn = width * jax.random.normal(key, shape, jnp.float32)
    if shards:
        drawn = drawn * steps_of(key, shape, shards, -0.22, 0.18)
    return jnp.clip(drawn, -most, most).astype(kind)


def setup_inputs(seed: int = 0) -> dict:
    key_list = jax.random.split(jax.random.key(seed), 7)
    inputs = centred(key_list[0], (TOKENS, D), 1.0, 6.0, ((0, 128), (1, 4)))
    out_grad = centred(key_list[1], (TOKENS, D), 0.5, 3.0, ((0, 128), (1, 4)))
    gate_weights = jnp.clip(jnp.exp(math.log(0.6) - 2.4849067 * jax.random.uniform(key_list[2], (TOKENS, TOP), jnp.float32) ** steps_of(key_list[2], (TOKENS, TOP), ((0, 128),), -0.2, 0.2)), 0.05, 0.6)
    routes_keys = jax.random.split(jax.random.fold_in(key_list[3], 1), TOKENS // TOK_DEV)
    routes_turns = jax.random.permutation(jax.random.fold_in(key_list[3], 3), TOKENS // TOK_DEV)
    routes = jax.vmap(lambda own, number: shared_out(jax.random.fold_in(key_list[3], 2), own, number, TOK_DEV, EXPERTS, TOP, CAP, 2))(routes_keys, routes_turns).reshape((TOKENS, TOP))
    up_weight = centred(key_list[4], (EXPERTS, H, D), D ** -0.5, 0.125, ((0, 128), (1, 4)))
    down_weight = centred(key_list[5], (EXPERTS, H, D), H ** -0.5, 0.21875, ((0, 128), (1, 4)))
    return {"inputs": inputs, "out_grad": out_grad, "gate_weights": gate_weights, "routes": routes, "up_weight": up_weight, "down_weight": down_weight}


def slot_rows(routes):
    block_count = TOKENS // TOK_DEV
    blocks = routes.reshape(block_count, TOK_DEV * TOP)
    onehot = (blocks[:, :, None] == jnp.arange(EXPERTS, dtype=jnp.int32)[None, None, :]).astype(jnp.int32)
    earlier = jnp.cumsum(onehot, axis=1) - onehot
    ranks = jnp.sum(earlier * onehot, axis=2)
    base = jnp.arange(block_count, dtype=jnp.int32)[:, None] * CAP
    return (base + ranks).reshape(-1).astype(jnp.int32)


def reference(inputs, out_grad, gate_weights, routes, up_weight, down_weight):
    flat_routes = routes.reshape(-1).astype(jnp.int32)
    route_row = slot_rows(routes)
    route_total = TOKENS * TOP
    row_total = EXPERTS * CAP
    x_padded = jnp.concatenate([inputs, jnp.zeros((1, D), inputs.dtype)], axis=0)
    out_padded = jnp.concatenate([out_grad, jnp.zeros((1, D), out_grad.dtype)], axis=0)
    gate_padded = jnp.concatenate([gate_weights.reshape(-1), jnp.zeros((1,), jnp.float32)])
    route_ids = jnp.arange(route_total, dtype=jnp.int32)

    def per_expert(accum, items):
        expert_id, up_mat, down_mat = items
        target = jnp.where(flat_routes == expert_id, route_row, row_total).astype(jnp.int32)
        route_of = jnp.full((row_total,), route_total, jnp.int32).at[target].set(route_ids, mode="drop")
        token_idx = jnp.where(route_of < route_total, route_of // TOP, TOKENS).astype(jnp.int32)
        in_rows = x_padded[token_idx]
        gate_rows = gate_padded[route_of]
        grad_rows = (gate_rows[:, None] * out_padded[token_idx].astype(jnp.float32)).astype(jnp.bfloat16)
        pre = jnp.dot(in_rows, up_mat.T, preferred_element_type=jnp.float32)
        sigma = jax.nn.sigmoid(pre)
        hidden = (pre * sigma).astype(jnp.bfloat16)
        back = jnp.dot(grad_rows, down_mat.T, preferred_element_type=jnp.float32)
        d_pre = (back * sigma * (1.0 + pre * (1.0 - sigma))).astype(jnp.bfloat16)
        grad_up = jnp.dot(d_pre.T, in_rows, preferred_element_type=jnp.float32).astype(jnp.bfloat16)
        grad_down = jnp.dot(hidden.T, grad_rows, preferred_element_type=jnp.float32).astype(jnp.bfloat16)
        quarters = jnp.einsum("rqj,qjd->qrd", d_pre.reshape(row_total, N_DP, HQ).astype(jnp.float32), up_mat.reshape(N_DP, HQ, D).astype(jnp.float32))
        rounded = lax.optimization_barrier(quarters.astype(jnp.bfloat16))
        total = jnp.sum(rounded.astype(jnp.float32), axis=0)
        accum = accum.at[token_idx].add(total, mode="drop")
        return accum, (grad_up, grad_down)

    start = jnp.zeros((TOKENS, D), jnp.float32)
    accum, grads = lax.scan(per_expert, start, (jnp.arange(EXPERTS, dtype=jnp.int32), up_weight, down_weight))
    return accum.astype(jnp.bfloat16), grads[0], grads[1]
```

```python
import jax
import jax.numpy as jnp
from jax import lax
from jax.sharding import PartitionSpec as P

F32 = jnp.float32
BF16 = jnp.bfloat16
CONTRACT_LAST = (((1,), (1,)), ((), ()))
CONTRACT_FIRST = (((0,), (0,)), ((), ()))


def route_masks(routes, gate_weights, expert_count, capacity):
    token_count = routes.shape[0]
    experts = lax.broadcasted_iota(jnp.int32, (expert_count, token_count), 0)
    match = jnp.zeros((expert_count, token_count), jnp.bool_)
    gates = jnp.zeros((expert_count, token_count), F32)
    for k in range(routes.shape[1]):
        hit = routes[:, k][None, :] == experts
        match = match | hit
        gates = gates + jnp.where(hit, gate_weights[:, k][None, :], 0.0)
    before = lax.broadcasted_iota(jnp.int32, (token_count, token_count), 0)
    after = lax.broadcasted_iota(jnp.int32, (token_count, token_count), 1)
    ranks = jnp.dot(
        match.astype(BF16), (before < after).astype(BF16), preferred_element_type=F32
    ).astype(jnp.int32)
    slots = jnp.arange(capacity, dtype=jnp.int32)
    chosen = match[:, None, :] & (ranks[:, None, :] == slots[None, :, None])
    slot_gates = jnp.sum(jnp.where(chosen, gates[:, None, :], 0.0), axis=2)
    chosen = chosen.reshape(expert_count * capacity, token_count).astype(BF16)
    return chosen, slot_gates.reshape(expert_count * capacity, 1)


def local(inputs, out_grad, gate_weights, routes, up_weight, down_weight):
    expert_count = lax.axis_size("expert")
    dp_count = lax.axis_size("dp")
    token_count, route_count = routes.shape
    capacity = max(2, token_count * route_count * 2 // expert_count)
    per_dev = capacity // dp_count
    rows = expert_count * per_dev
    part = inputs.shape[1]
    width = part * dp_count
    peers = expert_count * dp_count

    up_full = lax.all_gather(up_weight[0], "dp", axis=0, tiled=True)
    down_full = lax.all_gather(down_weight[0], "dp", axis=0, tiled=True)

    chosen, slot_gates = route_masks(routes, gate_weights, expert_count, capacity)

    def swap(values):
        return lax.all_to_all(values, ("expert", "dp"), split_axis=0, concat_axis=0, tiled=True)

    send_in = jnp.dot(chosen, inputs, preferred_element_type=F32).astype(BF16)
    scaled = slot_gates * jnp.dot(chosen, out_grad, preferred_element_type=F32)
    send_grad = scaled.astype(BF16)
    both = jnp.concatenate(
        [send_in.reshape(peers, per_dev, part), send_grad.reshape(peers, per_dev, part)], axis=1
    )
    both = swap(both).reshape(expert_count, dp_count, 2, per_dev, part)
    both = both.transpose(2, 0, 3, 1, 4).reshape(2, rows, width)
    in_rows, grad_rows = both[0], both[1]

    pre = lax.dot_general(in_rows, up_full, CONTRACT_LAST, preferred_element_type=F32)
    sigma = jax.nn.sigmoid(pre)
    hidden = (pre * sigma).astype(BF16)
    back = lax.dot_general(grad_rows, down_full, CONTRACT_LAST, preferred_element_type=F32)
    d_pre = (back * sigma * (1.0 + pre * (1.0 - sigma))).astype(BF16)

    back_rows = jnp.dot(d_pre, up_full, preferred_element_type=F32).astype(BF16)
    back_rows = back_rows.reshape(expert_count, per_dev, dp_count, part).transpose(0, 2, 1, 3)
    returned = swap(back_rows.reshape(peers, per_dev, part))
    returned = returned.reshape(peers * per_dev, part)

    def weight_grad(left, right):
        total = lax.dot_general(left, right, CONTRACT_FIRST, preferred_element_type=F32)
        return total.astype(BF16).reshape(dp_count, 1, -1, width)

    grads = jnp.concatenate([weight_grad(d_pre, in_rows), weight_grad(hidden, grad_rows)], axis=1)
    grads = lax.psum_scatter(grads, "dp", scatter_dimension=0, tiled=False)

    in_grad = lax.dot_general(chosen, returned, CONTRACT_FIRST, preferred_element_type=F32)
    return (in_grad.astype(BF16), grads[0][None], grads[1][None])


def solution(mesh):
    return jax.shard_map(
        local,
        mesh=mesh,
        in_specs=(
            P("expert", "dp"),
            P("expert", "dp"),
            P("expert", None),
            P("expert", None),
            P("expert", "dp", None),
            P("expert", "dp", None),
        ),
        out_specs=(P("expert", "dp"), P("expert", "dp", None), P("expert", "dp", None)),
        check_vma=False,
    )
```

```python
import jax
import jax.numpy as jnp
from jax import lax
from jax.experimental import pallas as pl
from jax.experimental.pallas import tpu as pltpu
from jax.sharding import PartitionSpec as P

F32 = jnp.float32
BF16 = jnp.bfloat16
I32 = jnp.int32
CONTRACT_LAST = (((1,), (1,)), ((), ()))
CONTRACT_FIRST = (((0,), (0,)), ((), ()))
BLOCK = 256
VMEM_LIMIT = 56 * 1024 * 1024


def bits(values, low, count):
    return (values >> low) & ((1 << count) - 1)


def row_permutation(source_of):
    row = lax.broadcasted_iota(I32, (BLOCK, BLOCK), 0)
    col = lax.broadcasted_iota(I32, (BLOCK, BLOCK), 1)
    return (col == source_of(row)).astype(F32).astype(BF16)


def pick(matrix, values):
    return jnp.dot(matrix, values, preferred_element_type=F32).astype(BF16)


def send_source(i):
    e, q, h, a, r = bits(i, 5, 3), bits(i, 3, 2), bits(i, 2, 1), bits(i, 1, 1), bits(i, 0, 1)
    return a * 128 + h * 64 + e * 8 + q * 2 + r


def lanes_source(i):
    g, e, r = bits(i, 4, 4), bits(i, 1, 3), bits(i, 0, 1)
    return e * 32 + g * 2 + r


def rows_source(i):
    e, g, r = bits(i, 5, 3), bits(i, 1, 4), bits(i, 0, 1)
    return g * 16 + e * 2 + r


def final_source(i):
    f, e, q, r = bits(i, 6, 2), bits(i, 3, 3), bits(i, 1, 2), bits(i, 0, 1)
    return e * 32 + q * 8 + f * 2 + r


def dispatch_kernel(routes_ref, gates_ref, in_ref, out_ref, send_ref, chosen_ref, nat_in, nat_grad):
    route_count, tokens = routes_ref.shape
    slot_rows = chosen_ref.shape[0]
    capacity = 8
    experts = slot_rows // capacity
    expert_id = lax.broadcasted_iota(I32, (experts, tokens), 0)
    match = jnp.zeros((experts, tokens), F32)
    gates = jnp.zeros((experts, tokens), F32)
    for k in range(route_count):
        hit = routes_ref[k : k + 1, :] == expert_id
        match = jnp.where(hit, 1.0, match)
        gates = jnp.where(hit, gates_ref[k : k + 1, :], gates)
    before = lax.broadcasted_iota(I32, (tokens, tokens), 0)
    after = lax.broadcasted_iota(I32, (tokens, tokens), 1)
    earlier = jnp.where(before < after, 1.0, 0.0).astype(BF16)
    ranks = jnp.dot(match.astype(BF16), earlier, preferred_element_type=F32)
    ranks = jnp.where(match > 0.0, ranks, -1.0)
    slot = lax.broadcasted_iota(I32, (experts, capacity, tokens), 1).astype(F32)
    chosen = jnp.where(ranks[:, None, :] == slot, 1.0, 0.0)
    slot_gates = jnp.sum((chosen * gates[:, None, :]).reshape(slot_rows, tokens), axis=1, keepdims=True)
    chosen = chosen.reshape(slot_rows, tokens).astype(BF16)
    chosen_ref[...] = chosen
    nat_in[...] = jnp.dot(chosen, in_ref[...], preferred_element_type=F32).astype(BF16)
    scaled = slot_gates * jnp.dot(chosen, out_ref[...], preferred_element_type=F32)
    nat_grad[...] = scaled.astype(BF16)
    order = row_permutation(send_source)
    for blk in range(send_ref.shape[0] // BLOCK):
        at = slice(blk * 64, blk * 64 + 64)
        parts = [nat[at, h * BLOCK : h * BLOCK + BLOCK] for nat in (nat_in, nat_grad) for h in (0, 1)]
        send_ref[blk * BLOCK : blk * BLOCK + BLOCK, :] = pick(order, jnp.concatenate(parts, axis=0))


def expert_kernel(
    recv_ref, u0, u1, u2, u3, d0, d1, d2, d3,
    ret_ref, own_out, first_p, first_m, plain_p, plain_m, held_p, held_m,
    up, down, in_rows, grad_rows, own_s, fp_s, fm_s, pp_s, pm_s, hp_s, hm_s, sems, out_sems,
):
    part = u0.shape[0]
    half = part // 2
    copies = []
    for i, (ref, full) in enumerate(
        [(r, up) for r in (u0, u1, u2, u3)] + [(r, down) for r in (d0, d1, d2, d3)]
    ):
        at = (i % 4) * part
        copies.append(pltpu.make_async_copy(ref, full.at[pl.ds(at, part), :], sems.at[i]))
        copies[-1].start()
    to_lanes = row_permutation(lanes_source)
    for blk in range(recv_ref.shape[0] // BLOCK):
        moved = pick(to_lanes, recv_ref[blk * BLOCK : blk * BLOCK + BLOCK, :])
        for g in range(8):
            for a, rows in ((0, in_rows), (1, grad_rows)):
                rows[blk * 16 : blk * 16 + 16, g * BLOCK : g * BLOCK + BLOCK] = moved[
                    (2 * g + a) * 16 : (2 * g + a) * 16 + 16, :
                ]
    for copy in copies[:4]:
        copy.wait()
    pre = lax.dot_general(up[...], in_rows[...], CONTRACT_LAST, preferred_element_type=F32)
    for copy in copies[4:]:
        copy.wait()
    back = lax.dot_general(down[...], grad_rows[...], CONTRACT_LAST, preferred_element_type=F32)
    sigma = jax.nn.sigmoid(pre)
    hidden = (pre * sigma).astype(BF16)
    d_pre = (back * sigma * (1.0 + pre * (1.0 - sigma))).astype(BF16)

    width = in_rows.shape[1]
    step = 512
    for w, (left, rows) in enumerate(((d_pre, in_rows), (hidden, grad_rows))):
        for n in range(width // step):
            lanes = slice(n * step, n * step + step)
            total = jnp.dot(left, rows[:, lanes], preferred_element_type=F32).astype(BF16)
            one, two = slice(w * half, w * half + half), slice(w * part, w * part + part)
            own_s[two, lanes] = total[:part]
            hp_s[one, lanes] = total[part : part + half]
            pp_s[one, lanes] = total[part + half : 2 * part]
            pm_s[one, lanes] = total[2 * part : 2 * part + half]
            hm_s[one, lanes] = total[2 * part + half : 3 * part]
            fp_s[one, lanes] = total[3 * part : 3 * part + half]
            fm_s[one, lanes] = total[3 * part + half :]
    outs = []
    for i, (src, dst) in enumerate(
        (
            (fp_s, first_p), (fm_s, first_m), (pp_s, plain_p), (pm_s, plain_m),
            (hp_s, held_p), (hm_s, held_m), (own_s, own_out),
        )
    ):
        outs.append(pltpu.make_async_copy(src, dst, out_sems.at[i]))
        outs[-1].start()

    rows_back = lax.dot_general(d_pre, up[...], CONTRACT_FIRST, preferred_element_type=F32)
    rows_back = rows_back.astype(BF16)
    to_rows = row_permutation(rows_source)
    for blk in range(ret_ref.shape[0] // BLOCK):
        parts = [rows_back[blk * 16 : blk * 16 + 16, g * 128 : g * 128 + 128] for g in range(16)]
        ret_ref[blk * BLOCK : blk * BLOCK + BLOCK, :] = pick(to_rows, jnp.concatenate(parts, axis=0))
    for copy in outs:
        copy.wait()


def combine_kernel(recv_ref, chosen_ref, out_ref, rows):
    order = row_permutation(final_source)
    for blk in range(recv_ref.shape[0] // BLOCK):
        moved = pick(order, recv_ref[blk * BLOCK : blk * BLOCK + BLOCK, :])
        for f in range(4):
            rows[blk * 64 : blk * 64 + 64, f * 128 : f * 128 + 128] = moved[f * 64 : f * 64 + 64, :]
    total = lax.dot_general(
        chosen_ref[...], rows[...], CONTRACT_FIRST, preferred_element_type=F32
    )
    out_ref[...] = total.astype(BF16)


def grads_kernel(own, last_p, last_m, plain_p, plain_m, up_out, down_out):
    half = last_p.shape[0] // 2
    for w, out in enumerate((up_out, down_out)):
        one = slice(w * half, w * half + half)
        low = slice(2 * w * half, 2 * w * half + half)
        high = slice(2 * w * half + half, 2 * w * half + 2 * half)
        out[:half, :] = (
            own[low, :].astype(F32) + last_p[one, :].astype(F32) + plain_m[one, :].astype(F32)
        ).astype(BF16)
        out[half:, :] = (
            own[high, :].astype(F32) + plain_p[one, :].astype(F32) + last_m[one, :].astype(F32)
        ).astype(BF16)


def shape(dims, dtype=BF16):
    return jax.ShapeDtypeStruct(dims, dtype)


PARAMS = pltpu.CompilerParams(vmem_limit_bytes=VMEM_LIMIT)


def local(inputs, out_grad, gate_weights, routes, up_weight, down_weight):
    expert_count = lax.axis_size("expert")
    dp_count = lax.axis_size("dp")
    token_count, route_count = routes.shape
    capacity = 8
    slot_rows = expert_count * capacity
    row_count = slot_rows // dp_count
    part = inputs.shape[1]
    width = part * dp_count
    peers = expert_count * dp_count
    hidden_part = up_weight.shape[1]
    hidden = hidden_part * dp_count
    half = hidden_part // 2

    def shift(value, by):
        pairs = [(i, (i + by) % dp_count) for i in range(dp_count)]
        return lax.ppermute(value, "dp", pairs)

    def swap(values):
        lanes = values.shape[1]
        moved = lax.all_to_all(
            values.reshape(peers, 8, lanes), ("expert", "dp"), split_axis=0, concat_axis=0, tiled=True
        )
        return moved.reshape(peers * 8, lanes)

    send, chosen = pl.pallas_call(
        dispatch_kernel,
        out_shape=(shape((slot_rows * 4, BLOCK)), shape((slot_rows, token_count))),
        scratch_shapes=[pltpu.VMEM((slot_rows, part), BF16), pltpu.VMEM((slot_rows, part), BF16)],
        compiler_params=PARAMS,
        name="dispatch",
    )(routes.T, gate_weights.T, inputs, out_grad)
    recv = swap(send)

    up_own, down_own = up_weight[0], down_weight[0]
    ups = [up_own] + [shift(up_own, by) for by in (-1, 1, 2)]
    downs = [down_own] + [shift(down_own, by) for by in (-1, 1, 2)]

    any_spec = pl.BlockSpec(memory_space=pl.ANY)
    vmem_spec = pl.BlockSpec(memory_space=pltpu.VMEM)
    piece = shape((hidden_part, width))
    whole = shape((2 * hidden_part, width))
    ret, own, first_p, first_m, plain_p, plain_m, held_p, held_m = pl.pallas_call(
        expert_kernel,
        in_specs=[vmem_spec] + [any_spec] * 8,
        out_specs=(vmem_spec,) + (any_spec,) * 7,
        out_shape=(shape((slot_rows * 4, 128)), whole) + (piece,) * 6,
        scratch_shapes=[
            pltpu.VMEM((hidden, width), BF16),
            pltpu.VMEM((hidden, width), BF16),
            pltpu.VMEM((row_count, width), BF16),
            pltpu.VMEM((row_count, width), BF16),
            pltpu.VMEM((2 * hidden_part, width), BF16),
        ]
        + [pltpu.VMEM((hidden_part, width), BF16)] * 6
        + [pltpu.SemaphoreType.DMA((8,)), pltpu.SemaphoreType.DMA((7,))],
        compiler_params=PARAMS,
        name="expert",
    )(recv, *ups, *downs)

    got_p, got_m = shift(first_p, 1), shift(first_m, -1)
    returned = swap(ret)
    plain_p, plain_m = shift(plain_p, 1), shift(plain_m, -1)
    last_p = shift((held_p.astype(F32) + got_p.astype(F32)).astype(BF16), 1)
    last_m = shift((held_m.astype(F32) + got_m.astype(F32)).astype(BF16), -1)
    grad_up, grad_down = pl.pallas_call(
        grads_kernel,
        out_shape=(piece, piece),
        compiler_params=PARAMS,
        name="grads",
    )(own, last_p, last_m, plain_p, plain_m)

    in_grad = pl.pallas_call(
        combine_kernel,
        out_shape=shape((token_count, part)),
        scratch_shapes=[pltpu.VMEM((slot_rows, part), BF16)],
        compiler_params=PARAMS,
        name="combine",
    )(returned, chosen)
    return (in_grad, grad_up[None], grad_down[None])


def solution(mesh):
    return jax.shard_map(
        local,
        mesh=mesh,
        in_specs=(
            P("expert", "dp"),
            P("expert", "dp"),
            P("expert", None),
            P("expert", None),
            P("expert", "dp", None),
            P("expert", "dp", None),
        ),
        out_specs=(P("expert", "dp"), P("expert", "dp", None), P("expert", "dp", None)),
        check_vma=False,
    )
```

```python
import jax
import jax.numpy as jnp
from jax import lax
from jax.experimental import pallas as pl
from jax.experimental.pallas import tpu as pltpu
from jax.sharding import PartitionSpec as P

F32 = jnp.float32
BF16 = jnp.bfloat16
I32 = jnp.int32
CONTRACT_LAST = (((1,), (1,)), ((), ()))
CONTRACT_FIRST = (((0,), (0,)), ((), ()))
BLOCK = 256
VMEM_LIMIT = 32 * 1024 * 1024


def bits(values, low, count):
    return (values >> low) & ((1 << count) - 1)


def row_permutation(source_of):
    row = lax.broadcasted_iota(I32, (BLOCK, BLOCK), 0)
    col = lax.broadcasted_iota(I32, (BLOCK, BLOCK), 1)
    return (col == source_of(row)).astype(F32).astype(BF16)


def pick(matrix, values):
    return jnp.dot(matrix, values, preferred_element_type=F32).astype(BF16)


def send_source(i):
    e, q, h, a, r = bits(i, 5, 3), bits(i, 3, 2), bits(i, 2, 1), bits(i, 1, 1), bits(i, 0, 1)
    return a * 128 + h * 64 + e * 8 + q * 2 + r


def lanes_source(i):
    g, e, r = bits(i, 4, 4), bits(i, 1, 3), bits(i, 0, 1)
    return e * 32 + g * 2 + r


def rows_source(i):
    e, g, r = bits(i, 5, 3), bits(i, 1, 4), bits(i, 0, 1)
    return g * 16 + e * 2 + r


def final_source(i):
    f, e, q, r = bits(i, 6, 2), bits(i, 3, 3), bits(i, 1, 2), bits(i, 0, 1)
    return e * 32 + q * 8 + f * 2 + r


CHUNKS = 4


def chunk_copy(src, dst, sems, i):
    rows = src.shape[0] // CHUNKS
    at = pl.ds(i * rows, rows)
    return pltpu.make_async_copy(src.at[at, :], dst.at[at, :], sems.at[i])


def drain(src, dst, sems, blk):
    per_chunk = src.shape[0] // BLOCK // CHUNKS
    if (blk + 1) % per_chunk == 0:
        chunk_copy(src, dst, sems, blk // per_chunk).start()


def finish(src, dst, sems):
    for i in range(CHUNKS):
        chunk_copy(src, dst, sems, i).wait()


def dispatch_kernel(
    routes_ref, gates_ref, in_ref, out_ref, send_hbm, chosen_ref, send_ref, nat_in, nat_grad, sems
):
    route_count, tokens = routes_ref.shape
    slot_rows = chosen_ref.shape[0]
    capacity = 8
    experts = slot_rows // capacity
    expert_id = lax.broadcasted_iota(I32, (experts, tokens), 0)
    match = jnp.zeros((experts, tokens), F32)
    gates = jnp.zeros((experts, tokens), F32)
    for k in range(route_count):
        hit = routes_ref[k : k + 1, :] == expert_id
        match = jnp.where(hit, 1.0, match)
        gates = jnp.where(hit, gates_ref[k : k + 1, :], gates)
    before = lax.broadcasted_iota(I32, (tokens, tokens), 0)
    after = lax.broadcasted_iota(I32, (tokens, tokens), 1)
    earlier = jnp.where(before < after, 1.0, 0.0).astype(BF16)
    ranks = jnp.dot(match.astype(BF16), earlier, preferred_element_type=F32)
    ranks = jnp.where(match > 0.0, ranks, -1.0)
    slot = lax.broadcasted_iota(I32, (experts, capacity, tokens), 1).astype(F32)
    chosen = jnp.where(ranks[:, None, :] == slot, 1.0, 0.0)
    slot_gates = jnp.sum((chosen * gates[:, None, :]).reshape(slot_rows, tokens), axis=1, keepdims=True)
    chosen = chosen.reshape(slot_rows, tokens).astype(BF16)
    chosen_ref[...] = chosen
    nat_in[...] = jnp.dot(chosen, in_ref[...], preferred_element_type=F32).astype(BF16)
    scaled = slot_gates * jnp.dot(chosen, out_ref[...], preferred_element_type=F32)
    nat_grad[...] = scaled.astype(BF16)
    order = row_permutation(send_source)
    for blk in range(send_ref.shape[0] // BLOCK):
        at = slice(blk * 64, blk * 64 + 64)
        parts = [nat[at, h * BLOCK : h * BLOCK + BLOCK] for nat in (nat_in, nat_grad) for h in (0, 1)]
        send_ref[blk * BLOCK : blk * BLOCK + BLOCK, :] = pick(order, jnp.concatenate(parts, axis=0))
        drain(send_ref, send_hbm, sems, blk)
    finish(send_ref, send_hbm, sems)


def expert_kernel(
    recv_ref, u0, u1, u2, u3, d0, d1, d2, d3,
    d_pre_ref, up, own_out, first_p, first_m, plain_p, plain_m, held_p, held_m,
    down, in_rows, grad_rows, own_s, fp_s, fm_s, pp_s, pm_s, hp_s, hm_s, sems, out_sems,
):
    part = u0.shape[0]
    half = part // 2
    copies = []
    for i, (ref, full) in enumerate(
        [(r, up) for r in (u0, u1, u2, u3)] + [(r, down) for r in (d0, d1, d2, d3)]
    ):
        at = (i % 4) * part
        copies.append(pltpu.make_async_copy(ref, full.at[pl.ds(at, part), :], sems.at[i]))
        copies[-1].start()
    to_lanes = row_permutation(lanes_source)
    for blk in range(recv_ref.shape[0] // BLOCK):
        moved = pick(to_lanes, recv_ref[blk * BLOCK : blk * BLOCK + BLOCK, :])
        for g in range(8):
            for a, rows in ((0, in_rows), (1, grad_rows)):
                rows[blk * 16 : blk * 16 + 16, g * BLOCK : g * BLOCK + BLOCK] = moved[
                    (2 * g + a) * 16 : (2 * g + a) * 16 + 16, :
                ]
    for copy in copies[:4]:
        copy.wait()
    pre = lax.dot_general(up[...], in_rows[...], CONTRACT_LAST, preferred_element_type=F32)
    for copy in copies[4:]:
        copy.wait()
    back = lax.dot_general(down[...], grad_rows[...], CONTRACT_LAST, preferred_element_type=F32)
    sigma = jax.nn.sigmoid(pre)
    hidden = (pre * sigma).astype(BF16)
    d_pre = (back * sigma * (1.0 + pre * (1.0 - sigma))).astype(BF16)
    d_pre_ref[...] = d_pre

    outs = []

    def send(i, src, dst):
        outs.append(pltpu.make_async_copy(src, dst, out_sems.at[i]))
        outs[-1].start()

    width = in_rows.shape[1]
    step = 512
    for top in (3 * part, 2 * part, part, 0):
        for w, (left, rows) in enumerate(((d_pre, in_rows), (hidden, grad_rows))):
            one, two = slice(w * half, w * half + half), slice(w * part, w * part + part)
            for n in range(width // step):
                lanes = slice(n * step, n * step + step)
                total = jnp.dot(
                    left[top : top + part], rows[:, lanes], preferred_element_type=F32
                ).astype(BF16)
                if top == 0:
                    own_s[two, lanes] = total
                elif top == part:
                    hp_s[one, lanes] = total[:half]
                    pp_s[one, lanes] = total[half:]
                elif top == 2 * part:
                    pm_s[one, lanes] = total[:half]
                    hm_s[one, lanes] = total[half:]
                else:
                    fp_s[one, lanes] = total[:half]
                    fm_s[one, lanes] = total[half:]
        if top == 0:
            send(6, own_s, own_out)
        elif top == part:
            send(4, hp_s, held_p)
            send(2, pp_s, plain_p)
        elif top == 2 * part:
            send(3, pm_s, plain_m)
            send(5, hm_s, held_m)
        else:
            send(0, fp_s, first_p)
            send(1, fm_s, first_m)
    for copy in outs:
        copy.wait()


def return_kernel(d_pre_ref, up_ref, ret_hbm, ret_ref, sems):
    rows_back = lax.dot_general(
        d_pre_ref[...], up_ref[...], CONTRACT_FIRST, preferred_element_type=F32
    ).astype(BF16)
    to_rows = row_permutation(rows_source)
    for blk in range(ret_ref.shape[0] // BLOCK):
        parts = [rows_back[blk * 16 : blk * 16 + 16, g * 128 : g * 128 + 128] for g in range(16)]
        ret_ref[blk * BLOCK : blk * BLOCK + BLOCK, :] = pick(to_rows, jnp.concatenate(parts, axis=0))
        drain(ret_ref, ret_hbm, sems, blk)
    finish(ret_ref, ret_hbm, sems)


def combine_kernel(recv_ref, chosen_ref, out_ref, rows):
    order = row_permutation(final_source)
    for blk in range(recv_ref.shape[0] // BLOCK):
        moved = pick(order, recv_ref[blk * BLOCK : blk * BLOCK + BLOCK, :])
        for f in range(4):
            rows[blk * 64 : blk * 64 + 64, f * 128 : f * 128 + 128] = moved[f * 64 : f * 64 + 64, :]
    total = lax.dot_general(
        chosen_ref[...], rows[...], CONTRACT_FIRST, preferred_element_type=F32
    )
    out_ref[...] = total.astype(BF16)


def grads_kernel(own, last_p, last_m, plain_p, plain_m, up_out, down_out):
    half = last_p.shape[0] // 2
    for w, out in enumerate((up_out, down_out)):
        one = slice(w * half, w * half + half)
        low = slice(2 * w * half, 2 * w * half + half)
        high = slice(2 * w * half + half, 2 * w * half + 2 * half)
        out[:half, :] = (
            own[low, :].astype(F32) + last_p[one, :].astype(F32) + plain_m[one, :].astype(F32)
        ).astype(BF16)
        out[half:, :] = (
            own[high, :].astype(F32) + plain_p[one, :].astype(F32) + last_m[one, :].astype(F32)
        ).astype(BF16)


def shape(dims, dtype=BF16):
    return jax.ShapeDtypeStruct(dims, dtype)


def on_chip(dims):
    return pltpu.VMEM(dims, BF16)


def in_hbm(dims):
    return pltpu.HBM(dims, BF16)


def keep(value):
    return pltpu.with_memory_space_constraint(value, pltpu.VMEM)


PARAMS = pltpu.CompilerParams(vmem_limit_bytes=VMEM_LIMIT)


def local(inputs, out_grad, gate_weights, routes, up_weight, down_weight):
    expert_count = lax.axis_size("expert")
    dp_count = lax.axis_size("dp")
    token_count, route_count = routes.shape
    capacity = 8
    slot_rows = expert_count * capacity
    row_count = slot_rows // dp_count
    part = inputs.shape[1]
    width = part * dp_count
    peers = expert_count * dp_count
    hidden_part = up_weight.shape[1]
    hidden = hidden_part * dp_count
    half = hidden_part // 2

    def shift(value, by):
        pairs = [(i, (i + by) % dp_count) for i in range(dp_count)]
        return lax.ppermute(value, "dp", pairs)

    def swap(values):
        lanes = values.shape[1]
        moved = lax.all_to_all(
            values.reshape(peers, 8, lanes), ("expert", "dp"), split_axis=0, concat_axis=0, tiled=True
        )
        return moved.reshape(peers * 8, lanes)

    hbm = pl.BlockSpec(memory_space=pltpu.HBM)
    vmem = pl.BlockSpec(memory_space=pltpu.VMEM)
    send_rows = slot_rows * 4
    send, chosen = pl.pallas_call(
        dispatch_kernel,
        out_specs=(hbm, vmem),
        out_shape=(in_hbm((send_rows, BLOCK)), on_chip((slot_rows, token_count))),
        scratch_shapes=[
            pltpu.VMEM((send_rows, BLOCK), BF16),
            pltpu.VMEM((slot_rows, part), BF16),
            pltpu.VMEM((slot_rows, part), BF16),
            pltpu.SemaphoreType.DMA((CHUNKS,)),
        ],
        compiler_params=PARAMS,
        name="dispatch",
    )(routes.T, gate_weights.T, inputs, out_grad)
    recv = swap(send)

    up_own, down_own = up_weight[0], down_weight[0]
    ups = [up_own] + [shift(up_own, by) for by in (-1, 1, 2)]
    downs = [down_own] + [shift(down_own, by) for by in (-1, 1, 2)]
    weights = [pltpu.with_memory_space_constraint(value, pltpu.HBM) for value in ups + downs]

    piece = (hidden_part, width)
    whole = (2 * hidden_part, width)
    d_pre, up_full, own, first_p, first_m, plain_p, plain_m, held_p, held_m = pl.pallas_call(
        expert_kernel,
        in_specs=[vmem] + [hbm] * 8,
        out_specs=(vmem,) * 2 + (hbm,) * 7,
        out_shape=(on_chip((hidden, row_count)), on_chip((hidden, width)), in_hbm(whole))
        + (in_hbm(piece),) * 6,
        scratch_shapes=[pltpu.VMEM((hidden, width), BF16)]
        + [pltpu.VMEM((row_count, width), BF16)] * 2
        + [pltpu.VMEM(whole, BF16)]
        + [pltpu.VMEM(piece, BF16)] * 6
        + [pltpu.SemaphoreType.DMA((8,)), pltpu.SemaphoreType.DMA((7,))],
        compiler_params=PARAMS,
        name="expert",
    )(keep(recv), *weights)

    got_p, got_m = shift(first_p, 1), shift(first_m, -1)
    ret = pl.pallas_call(
        return_kernel,
        out_specs=hbm,
        out_shape=in_hbm((send_rows, 128)),
        scratch_shapes=[pltpu.VMEM((send_rows, 128), BF16), pltpu.SemaphoreType.DMA((CHUNKS,))],
        compiler_params=PARAMS,
        name="rows_back",
    )(keep(d_pre), keep(up_full))
    returned = swap(ret)
    plain_p, plain_m = shift(plain_p, 1), shift(plain_m, -1)
    last_p = shift((held_p.astype(F32) + got_p.astype(F32)).astype(BF16), 1)
    last_m = shift((held_m.astype(F32) + got_m.astype(F32)).astype(BF16), -1)
    grad_up, grad_down = pl.pallas_call(
        grads_kernel,
        out_shape=(shape(piece), shape(piece)),
        compiler_params=PARAMS,
        name="grads",
    )(keep(own), keep(last_p), keep(last_m), keep(plain_p), keep(plain_m))

    in_grad = pl.pallas_call(
        combine_kernel,
        out_shape=shape((token_count, part)),
        scratch_shapes=[pltpu.VMEM((slot_rows, part), BF16)],
        compiler_params=PARAMS,
        name="combine",
    )(keep(returned), keep(chosen))
    return (in_grad, grad_up[None], grad_down[None])


def solution(mesh):
    return jax.shard_map(
        local,
        mesh=mesh,
        in_specs=(
            P("expert", "dp"),
            P("expert", "dp"),
            P("expert", None),
            P("expert", None),
            P("expert", "dp", None),
            P("expert", "dp", None),
        ),
        out_specs=(P("expert", "dp"), P("expert", "dp", None), P("expert", "dp", None)),
        check_vma=False,
    )
```

```python
import jax
import jax.numpy as jnp
from jax import lax
from jax.experimental import pallas as pl
from jax.experimental.pallas import tpu as pltpu
from jax.sharding import PartitionSpec as P

F32 = jnp.float32
BF16 = jnp.bfloat16
I32 = jnp.int32
CONTRACT_LAST = (((1,), (1,)), ((), ()))
CONTRACT_FIRST = (((0,), (0,)), ((), ()))
BLOCK = 256
VMEM_LIMIT = 32 * 1024 * 1024


def bits(values, low, count):
    return (values >> low) & ((1 << count) - 1)


def row_permutation(source_of):
    row = lax.broadcasted_iota(I32, (BLOCK, BLOCK), 0)
    col = lax.broadcasted_iota(I32, (BLOCK, BLOCK), 1)
    return (col == source_of(row)).astype(F32).astype(BF16)


def pick(matrix, values):
    return jnp.dot(matrix, values, preferred_element_type=F32).astype(BF16)


def send_source(i):
    e, q, h, a, r = bits(i, 5, 3), bits(i, 3, 2), bits(i, 2, 1), bits(i, 1, 1), bits(i, 0, 1)
    return a * 128 + h * 64 + e * 8 + q * 2 + r


def lanes_source(i):
    g, e, r = bits(i, 4, 4), bits(i, 1, 3), bits(i, 0, 1)
    return e * 32 + g * 2 + r


def rows_source(i):
    e, g, r = bits(i, 5, 3), bits(i, 1, 4), bits(i, 0, 1)
    return g * 16 + e * 2 + r


def final_source(i):
    f, e, q, r = bits(i, 6, 2), bits(i, 3, 3), bits(i, 1, 2), bits(i, 0, 1)
    return e * 32 + q * 8 + f * 2 + r


CHUNKS = 4


def chunk_copy(src, dst, sems, i):
    rows = src.shape[0] // CHUNKS
    at = pl.ds(i * rows, rows)
    return pltpu.make_async_copy(src.at[at, :], dst.at[at, :], sems.at[i])


def drain(src, dst, sems, blk):
    per_chunk = src.shape[0] // BLOCK // CHUNKS
    if (blk + 1) % per_chunk == 0:
        chunk_copy(src, dst, sems, blk // per_chunk).start()


def finish(src, dst, sems):
    for i in range(CHUNKS):
        chunk_copy(src, dst, sems, i).wait()


def dispatch_kernel(
    routes_hbm, gates_hbm, in_hbm_ref, out_hbm_ref, send_hbm, chosen_ref,
    routes_ref, gates_ref, in_ref, out_ref, send_ref, nat_in, nat_grad, sems, in_sems,
):
    loads = [
        pltpu.make_async_copy(src, dst, in_sems.at[i])
        for i, (src, dst) in enumerate(
            (
                (routes_hbm, routes_ref), (gates_hbm, gates_ref),
                (in_hbm_ref, in_ref), (out_hbm_ref, out_ref),
            )
        )
    ]
    for load in loads:
        load.start()
    for load in loads[:2]:
        load.wait()
    route_count, tokens = routes_ref.shape
    slot_rows = chosen_ref.shape[0]
    capacity = 8
    experts = slot_rows // capacity
    expert_id = lax.broadcasted_iota(I32, (experts, tokens), 0)
    match = jnp.zeros((experts, tokens), F32)
    gates = jnp.zeros((experts, tokens), F32)
    for k in range(route_count):
        hit = routes_ref[k : k + 1, :] == expert_id
        match = jnp.where(hit, 1.0, match)
        gates = jnp.where(hit, gates_ref[k : k + 1, :], gates)
    before = lax.broadcasted_iota(I32, (tokens, tokens), 0)
    after = lax.broadcasted_iota(I32, (tokens, tokens), 1)
    earlier = jnp.where(before < after, 1.0, 0.0).astype(BF16)
    ranks = jnp.dot(match.astype(BF16), earlier, preferred_element_type=F32)
    ranks = jnp.where(match > 0.0, ranks, -1.0)
    slot = lax.broadcasted_iota(I32, (experts, capacity, tokens), 1).astype(F32)
    chosen = jnp.where(ranks[:, None, :] == slot, 1.0, 0.0)
    slot_gates = jnp.sum((chosen * gates[:, None, :]).reshape(slot_rows, tokens), axis=1, keepdims=True)
    chosen = chosen.reshape(slot_rows, tokens).astype(BF16)
    chosen_ref[...] = chosen
    for load in loads[2:]:
        load.wait()
    nat_in[...] = jnp.dot(chosen, in_ref[...], preferred_element_type=F32).astype(BF16)
    scaled = slot_gates * jnp.dot(chosen, out_ref[...], preferred_element_type=F32)
    nat_grad[...] = scaled.astype(BF16)
    order = row_permutation(send_source)
    for blk in range(send_ref.shape[0] // BLOCK):
        at = slice(blk * 64, blk * 64 + 64)
        parts = [nat[at, h * BLOCK : h * BLOCK + BLOCK] for nat in (nat_in, nat_grad) for h in (0, 1)]
        send_ref[blk * BLOCK : blk * BLOCK + BLOCK, :] = pick(order, jnp.concatenate(parts, axis=0))
        drain(send_ref, send_hbm, sems, blk)
    finish(send_ref, send_hbm, sems)


def expert_kernel(
    recv_ref, u0, u1, u2, u3, d0, d1, d2, d3,
    d_pre_ref, up, own_out, first_p, first_m, plain_p, plain_m, held_p, held_m,
    down, in_rows, grad_rows, own_s, fp_s, fm_s, pp_s, pm_s, hp_s, hm_s, sems, out_sems,
):
    part = u0.shape[0]
    half = part // 2
    copies = []
    for i, (ref, full) in enumerate(
        [(r, up) for r in (u0, u1, u2, u3)] + [(r, down) for r in (d0, d1, d2, d3)]
    ):
        at = (i % 4) * part
        copies.append(pltpu.make_async_copy(ref, full.at[pl.ds(at, part), :], sems.at[i]))
        copies[-1].start()
    to_lanes = row_permutation(lanes_source)
    for blk in range(recv_ref.shape[0] // BLOCK):
        moved = pick(to_lanes, recv_ref[blk * BLOCK : blk * BLOCK + BLOCK, :])
        for g in range(8):
            for a, rows in ((0, in_rows), (1, grad_rows)):
                rows[blk * 16 : blk * 16 + 16, g * BLOCK : g * BLOCK + BLOCK] = moved[
                    (2 * g + a) * 16 : (2 * g + a) * 16 + 16, :
                ]
    for copy in copies[:4]:
        copy.wait()
    pre = lax.dot_general(up[...], in_rows[...], CONTRACT_LAST, preferred_element_type=F32)
    for copy in copies[4:]:
        copy.wait()
    back = lax.dot_general(down[...], grad_rows[...], CONTRACT_LAST, preferred_element_type=F32)
    sigma = jax.nn.sigmoid(pre)
    hidden = (pre * sigma).astype(BF16)
    d_pre = (back * sigma * (1.0 + pre * (1.0 - sigma))).astype(BF16)
    d_pre_ref[...] = d_pre

    outs = []

    def send(i, src, dst):
        outs.append(pltpu.make_async_copy(src, dst, out_sems.at[i]))
        outs[-1].start()

    width = in_rows.shape[1]
    step = 512
    for top in (3 * part, 2 * part, part, 0):
        for w, (left, rows) in enumerate(((d_pre, in_rows), (hidden, grad_rows))):
            one, two = slice(w * half, w * half + half), slice(w * part, w * part + part)
            for n in range(width // step):
                lanes = slice(n * step, n * step + step)
                total = jnp.dot(
                    left[top : top + part], rows[:, lanes], preferred_element_type=F32
                ).astype(BF16)
                if top == 0:
                    own_s[two, lanes] = total
                elif top == part:
                    hp_s[one, lanes] = total[:half]
                    pp_s[one, lanes] = total[half:]
                elif top == 2 * part:
                    pm_s[one, lanes] = total[:half]
                    hm_s[one, lanes] = total[half:]
                else:
                    fp_s[one, lanes] = total[:half]
                    fm_s[one, lanes] = total[half:]
        if top == 0:
            send(6, own_s, own_out)
        elif top == part:
            send(4, hp_s, held_p)
            send(2, pp_s, plain_p)
        elif top == 2 * part:
            send(3, pm_s, plain_m)
            send(5, hm_s, held_m)
        else:
            send(0, fp_s, first_p)
            send(1, fm_s, first_m)
    for copy in outs:
        copy.wait()


def return_kernel(d_pre_ref, up_ref, ret_hbm, ret_ref, sems):
    rows_back = lax.dot_general(
        d_pre_ref[...], up_ref[...], CONTRACT_FIRST, preferred_element_type=F32
    ).astype(BF16)
    to_rows = row_permutation(rows_source)
    for blk in range(ret_ref.shape[0] // BLOCK):
        parts = [rows_back[blk * 16 : blk * 16 + 16, g * 128 : g * 128 + 128] for g in range(16)]
        ret_ref[blk * BLOCK : blk * BLOCK + BLOCK, :] = pick(to_rows, jnp.concatenate(parts, axis=0))
        drain(ret_ref, ret_hbm, sems, blk)
    finish(ret_ref, ret_hbm, sems)


def combine_kernel(recv_ref, chosen_ref, out_ref, rows):
    order = row_permutation(final_source)
    for blk in range(recv_ref.shape[0] // BLOCK):
        moved = pick(order, recv_ref[blk * BLOCK : blk * BLOCK + BLOCK, :])
        for f in range(4):
            rows[blk * 64 : blk * 64 + 64, f * 128 : f * 128 + 128] = moved[f * 64 : f * 64 + 64, :]
    total = lax.dot_general(
        chosen_ref[...], rows[...], CONTRACT_FIRST, preferred_element_type=F32
    )
    out_ref[...] = total.astype(BF16)


def grads_kernel(own, last_p, last_m, plain_p, plain_m, up_out, down_out):
    half = last_p.shape[0] // 2
    for w, out in enumerate((up_out, down_out)):
        one = slice(w * half, w * half + half)
        low = slice(2 * w * half, 2 * w * half + half)
        high = slice(2 * w * half + half, 2 * w * half + 2 * half)
        out[:half, :] = (
            own[low, :].astype(F32) + last_p[one, :].astype(F32) + plain_m[one, :].astype(F32)
        ).astype(BF16)
        out[half:, :] = (
            own[high, :].astype(F32) + plain_p[one, :].astype(F32) + last_m[one, :].astype(F32)
        ).astype(BF16)


def shape(dims, dtype=BF16):
    return jax.ShapeDtypeStruct(dims, dtype)


def on_chip(dims):
    return pltpu.VMEM(dims, BF16)


def in_hbm(dims):
    return pltpu.HBM(dims, BF16)


def keep(value):
    return pltpu.with_memory_space_constraint(value, pltpu.VMEM)


def leave(value):
    return pltpu.with_memory_space_constraint(value, pltpu.HBM)


PARAMS = pltpu.CompilerParams(vmem_limit_bytes=VMEM_LIMIT)


def local(inputs, out_grad, gate_weights, routes, up_weight, down_weight):
    expert_count = lax.axis_size("expert")
    dp_count = lax.axis_size("dp")
    token_count, route_count = routes.shape
    capacity = 8
    slot_rows = expert_count * capacity
    row_count = slot_rows // dp_count
    part = inputs.shape[1]
    width = part * dp_count
    peers = expert_count * dp_count
    hidden_part = up_weight.shape[1]
    hidden = hidden_part * dp_count
    half = hidden_part // 2

    def shift(value, by):
        pairs = [(i, (i + by) % dp_count) for i in range(dp_count)]
        return lax.ppermute(value, "dp", pairs)

    def swap(values):
        lanes = values.shape[1]
        moved = lax.all_to_all(
            values.reshape(peers, 8, lanes), ("expert", "dp"), split_axis=0, concat_axis=0, tiled=True
        )
        return moved.reshape(peers * 8, lanes)

    hbm = pl.BlockSpec(memory_space=pltpu.HBM)
    vmem = pl.BlockSpec(memory_space=pltpu.VMEM)
    send_rows = slot_rows * 4
    send, chosen = pl.pallas_call(
        dispatch_kernel,
        in_specs=[hbm] * 4,
        out_specs=(hbm, vmem),
        out_shape=(in_hbm((send_rows, BLOCK)), on_chip((slot_rows, token_count))),
        scratch_shapes=[
            pltpu.VMEM((route_count, token_count), I32),
            pltpu.VMEM((route_count, token_count), F32),
            pltpu.VMEM((token_count, part), BF16),
            pltpu.VMEM((token_count, part), BF16),
            pltpu.VMEM((send_rows, BLOCK), BF16),
            pltpu.VMEM((slot_rows, part), BF16),
            pltpu.VMEM((slot_rows, part), BF16),
            pltpu.SemaphoreType.DMA((CHUNKS,)),
            pltpu.SemaphoreType.DMA((4,)),
        ],
        compiler_params=PARAMS,
        name="dispatch",
    )(*[leave(value) for value in (routes.T, gate_weights.T, inputs, out_grad)])
    recv = swap(send)

    up_own, down_own = up_weight[0], down_weight[0]
    ups = [up_own] + [shift(up_own, by) for by in (-1, 1, 2)]
    downs = [down_own] + [shift(down_own, by) for by in (-1, 1, 2)]
    weights = [leave(value) for value in ups + downs]

    piece = (hidden_part, width)
    whole = (2 * hidden_part, width)
    d_pre, up_full, own, first_p, first_m, plain_p, plain_m, held_p, held_m = pl.pallas_call(
        expert_kernel,
        in_specs=[vmem] + [hbm] * 8,
        out_specs=(vmem,) * 2 + (hbm,) * 7,
        out_shape=(on_chip((hidden, row_count)), on_chip((hidden, width)), in_hbm(whole))
        + (in_hbm(piece),) * 6,
        scratch_shapes=[pltpu.VMEM((hidden, width), BF16)]
        + [pltpu.VMEM((row_count, width), BF16)] * 2
        + [pltpu.VMEM(whole, BF16)]
        + [pltpu.VMEM(piece, BF16)] * 6
        + [pltpu.SemaphoreType.DMA((8,)), pltpu.SemaphoreType.DMA((7,))],
        compiler_params=PARAMS,
        name="expert",
    )(keep(recv), *weights)

    got_p, got_m = shift(first_p, 1), shift(first_m, -1)
    ret = pl.pallas_call(
        return_kernel,
        out_specs=hbm,
        out_shape=in_hbm((send_rows, 128)),
        scratch_shapes=[pltpu.VMEM((send_rows, 128), BF16), pltpu.SemaphoreType.DMA((CHUNKS,))],
        compiler_params=PARAMS,
        name="rows_back",
    )(keep(d_pre), keep(up_full))
    returned = swap(ret)
    plain_p, plain_m = shift(plain_p, 1), shift(plain_m, -1)
    last_p = shift((held_p.astype(F32) + got_p.astype(F32)).astype(BF16), 1)
    last_m = shift((held_m.astype(F32) + got_m.astype(F32)).astype(BF16), -1)
    grad_up, grad_down = pl.pallas_call(
        grads_kernel,
        out_shape=(shape(piece), shape(piece)),
        compiler_params=PARAMS,
        cost_estimate=pl.CostEstimate(flops=3 * 10**10, transcendentals=0, bytes_accessed=6 * 10**6),
        name="grads",
    )(keep(own), keep(last_p), keep(last_m), keep(plain_p), keep(plain_m))

    in_grad = pl.pallas_call(
        combine_kernel,
        out_shape=shape((token_count, part)),
        scratch_shapes=[pltpu.VMEM((slot_rows, part), BF16)],
        compiler_params=PARAMS,
        name="combine",
    )(keep(returned), keep(chosen))
    return (in_grad, grad_up[None], grad_down[None])


def solution(mesh):
    return jax.shard_map(
        local,
        mesh=mesh,
        in_specs=(
            P("expert", "dp"),
            P("expert", "dp"),
            P("expert", None),
            P("expert", None),
            P("expert", "dp", None),
            P("expert", "dp", None),
        ),
        out_specs=(P("expert", "dp"), P("expert", "dp", None), P("expert", "dp", None)),
        check_vma=False,
    )
```

```python
import jax
import jax.numpy as jnp
from jax import lax
from jax.experimental import pallas as pl
from jax.experimental.pallas import tpu as pltpu
from jax.sharding import PartitionSpec as P

F32 = jnp.float32
BF16 = jnp.bfloat16
I32 = jnp.int32
CONTRACT_LAST = (((1,), (1,)), ((), ()))
CONTRACT_FIRST = (((0,), (0,)), ((), ()))
BLOCK = 256
VMEM_LIMIT = 32 * 1024 * 1024


def bits(values, low, count):
    return (values >> low) & ((1 << count) - 1)


def row_permutation(source_of):
    row = lax.broadcasted_iota(I32, (BLOCK, BLOCK), 0)
    col = lax.broadcasted_iota(I32, (BLOCK, BLOCK), 1)
    return (col == source_of(row)).astype(F32).astype(BF16)


def pick(matrix, values):
    return jnp.dot(matrix, values, preferred_element_type=F32).astype(BF16)


def send_source(i):
    e, q, h, a, r = bits(i, 5, 3), bits(i, 3, 2), bits(i, 2, 1), bits(i, 1, 1), bits(i, 0, 1)
    return a * 128 + h * 64 + e * 8 + q * 2 + r


def lanes_source(i):
    g, e, r = bits(i, 4, 4), bits(i, 1, 3), bits(i, 0, 1)
    return e * 32 + g * 2 + r


def rows_source(i):
    e, g, r = bits(i, 5, 3), bits(i, 1, 4), bits(i, 0, 1)
    return g * 16 + e * 2 + r


def final_source(i):
    f, e, q, r = bits(i, 6, 2), bits(i, 3, 3), bits(i, 1, 2), bits(i, 0, 1)
    return e * 32 + q * 8 + f * 2 + r


CHUNKS = 4


def chunk_copy(src, dst, sems, i):
    rows = src.shape[0] // CHUNKS
    at = pl.ds(i * rows, rows)
    return pltpu.make_async_copy(src.at[at, :], dst.at[at, :], sems.at[i])


def drain(src, dst, sems, blk):
    per_chunk = src.shape[0] // BLOCK // CHUNKS
    if (blk + 1) % per_chunk == 0:
        chunk_copy(src, dst, sems, blk // per_chunk).start()


def finish(src, dst, sems):
    for i in range(CHUNKS):
        chunk_copy(src, dst, sems, i).wait()


def dispatch_kernel(
    routes_hbm, gates_hbm, in_hbm_ref, out_hbm_ref, send_hbm, chosen_hbm,
    routes_ref, gates_ref, in_ref, out_ref, send_ref, chosen_ref, nat_in, nat_grad, sems, in_sems,
    chosen_sem,
):
    loads = [
        pltpu.make_async_copy(src, dst, in_sems.at[i])
        for i, (src, dst) in enumerate(
            (
                (routes_hbm, routes_ref), (gates_hbm, gates_ref),
                (in_hbm_ref, in_ref), (out_hbm_ref, out_ref),
            )
        )
    ]
    for load in loads:
        load.start()
    for load in loads[:2]:
        load.wait()
    route_count, tokens = routes_ref.shape
    slot_rows = chosen_ref.shape[0]
    capacity = 8
    experts = slot_rows // capacity
    expert_id = lax.broadcasted_iota(I32, (experts, tokens), 0)
    match = jnp.zeros((experts, tokens), F32)
    gates = jnp.zeros((experts, tokens), F32)
    for k in range(route_count):
        hit = routes_ref[k : k + 1, :] == expert_id
        match = jnp.where(hit, 1.0, match)
        gates = jnp.where(hit, gates_ref[k : k + 1, :], gates)
    before = lax.broadcasted_iota(I32, (tokens, tokens), 0)
    after = lax.broadcasted_iota(I32, (tokens, tokens), 1)
    earlier = jnp.where(before < after, 1.0, 0.0).astype(BF16)
    ranks = jnp.dot(match.astype(BF16), earlier, preferred_element_type=F32)
    ranks = jnp.where(match > 0.0, ranks, -1.0)
    slot = lax.broadcasted_iota(I32, (experts, capacity, tokens), 1).astype(F32)
    chosen = jnp.where(ranks[:, None, :] == slot, 1.0, 0.0)
    slot_gates = jnp.sum((chosen * gates[:, None, :]).reshape(slot_rows, tokens), axis=1, keepdims=True)
    chosen = chosen.reshape(slot_rows, tokens).astype(BF16)
    chosen_ref[...] = chosen
    save = pltpu.make_async_copy(chosen_ref, chosen_hbm, chosen_sem)
    save.start()
    for load in loads[2:]:
        load.wait()
    nat_in[...] = jnp.dot(chosen, in_ref[...], preferred_element_type=F32).astype(BF16)
    scaled = slot_gates * jnp.dot(chosen, out_ref[...], preferred_element_type=F32)
    nat_grad[...] = scaled.astype(BF16)
    order = row_permutation(send_source)
    for blk in range(send_ref.shape[0] // BLOCK):
        at = slice(blk * 64, blk * 64 + 64)
        parts = [nat[at, h * BLOCK : h * BLOCK + BLOCK] for nat in (nat_in, nat_grad) for h in (0, 1)]
        send_ref[blk * BLOCK : blk * BLOCK + BLOCK, :] = pick(order, jnp.concatenate(parts, axis=0))
        drain(send_ref, send_hbm, sems, blk)
    finish(send_ref, send_hbm, sems)
    save.wait()


def expert_kernel(
    recv_ref, u0, u1, u2, u3, d0, d1, d2, d3,
    d_pre_ref, up, hidden_hbm, d_pre_hbm, in_hbm_ref, grad_hbm_ref, first_p, first_m,
    down, hidden_ref, in_rows, grad_rows, fp_s, fm_s, sems, out_sems,
):
    part = u0.shape[0]
    half = part // 2
    copies = []
    for i, (ref, full) in enumerate(
        [(r, up) for r in (u0, u1, u2, u3)] + [(r, down) for r in (d0, d1, d2, d3)]
    ):
        at = (i % 4) * part
        copies.append(pltpu.make_async_copy(ref, full.at[pl.ds(at, part), :], sems.at[i]))
        copies[-1].start()
    to_lanes = row_permutation(lanes_source)
    for blk in range(recv_ref.shape[0] // BLOCK):
        moved = pick(to_lanes, recv_ref[blk * BLOCK : blk * BLOCK + BLOCK, :])
        for g in range(8):
            for a, rows in ((0, in_rows), (1, grad_rows)):
                rows[blk * 16 : blk * 16 + 16, g * BLOCK : g * BLOCK + BLOCK] = moved[
                    (2 * g + a) * 16 : (2 * g + a) * 16 + 16, :
                ]
    outs = []

    def save(src, dst):
        outs.append(pltpu.make_async_copy(src, dst, out_sems.at[len(outs)]))
        outs[-1].start()

    save(in_rows, in_hbm_ref)
    save(grad_rows, grad_hbm_ref)
    for copy in copies[:4]:
        copy.wait()
    pre = lax.dot_general(up[...], in_rows[...], CONTRACT_LAST, preferred_element_type=F32)
    for copy in copies[4:]:
        copy.wait()
    back = lax.dot_general(down[...], grad_rows[...], CONTRACT_LAST, preferred_element_type=F32)
    sigma = jax.nn.sigmoid(pre)
    hidden = (pre * sigma).astype(BF16)
    d_pre = (back * sigma * (1.0 + pre * (1.0 - sigma))).astype(BF16)
    d_pre_ref[...] = d_pre
    hidden_ref[...] = hidden
    save(d_pre_ref, d_pre_hbm)
    save(hidden_ref, hidden_hbm)
    top = 3 * part
    for w, (left, rows) in enumerate(((d_pre, in_rows), (hidden, grad_rows))):
        one = slice(w * half, w * half + half)
        for lanes in lane_steps(rows.shape[1]):
            total = part_grad(left[top:], rows, lanes)
            fp_s[one, lanes] = total[:half]
            fm_s[one, lanes] = total[half:]
    save(fp_s, first_p)
    save(fm_s, first_m)
    for copy in outs:
        copy.wait()


def lane_steps(width, step=512):
    return [slice(n, n + step) for n in range(0, width, step)]


def part_grad(left, rows, lanes):
    return jnp.dot(left, rows[:, lanes], preferred_element_type=F32).astype(BF16)


def rest_kernel(
    d_pre_hbm, hidden_hbm, in_hbm_ref, grad_hbm_ref,
    plain_p, plain_m, held_p, held_m, own_out,
    d_pre_ref, hidden_ref, in_rows, grad_rows, pp_s, pm_s, hp_s, hm_s, own_s, sems, in_sems,
):
    pairs = (
        (d_pre_hbm, d_pre_ref), (in_hbm_ref, in_rows), (hidden_hbm, hidden_ref), (grad_hbm_ref, grad_rows),
    )
    loads = [pltpu.make_async_copy(src, dst, in_sems.at[i]) for i, (src, dst) in enumerate(pairs)]
    for load in loads:
        load.start()
    for load in loads:
        load.wait()
    part = plain_p.shape[0]
    half = part // 2
    outs = []

    def send(src, dst):
        outs.append(pltpu.make_async_copy(src, dst, sems.at[len(outs)]))
        outs[-1].start()

    for piece in (1, 2, 0):
        for w, (left, rows) in enumerate(((d_pre_ref, in_rows), (hidden_ref, grad_rows))):
            one, two = slice(w * half, w * half + half), slice(w * part, w * part + part)
            mine = left[piece * part : piece * part + part, :]
            for lanes in lane_steps(rows.shape[1]):
                total = part_grad(mine, rows, lanes)
                if piece == 0:
                    own_s[two, lanes] = total
                else:
                    low, high = ((hp_s, pp_s), (pm_s, hm_s))[piece - 1]
                    low[one, lanes] = total[:half]
                    high[one, lanes] = total[half:]
        if piece == 0:
            send(own_s, own_out)
        elif piece == 1:
            send(pp_s, plain_p)
            send(hp_s, held_p)
        else:
            send(pm_s, plain_m)
            send(hm_s, held_m)
    for copy in outs:
        copy.wait()


def return_kernel(d_pre_ref, up_ref, ret_hbm, ret_ref, sems):
    rows_back = lax.dot_general(
        d_pre_ref[...], up_ref[...], CONTRACT_FIRST, preferred_element_type=F32
    ).astype(BF16)
    to_rows = row_permutation(rows_source)
    for blk in range(ret_ref.shape[0] // BLOCK):
        parts = [rows_back[blk * 16 : blk * 16 + 16, g * 128 : g * 128 + 128] for g in range(16)]
        ret_ref[blk * BLOCK : blk * BLOCK + BLOCK, :] = pick(to_rows, jnp.concatenate(parts, axis=0))
        drain(ret_ref, ret_hbm, sems, blk)
    finish(ret_ref, ret_hbm, sems)


def combine_kernel(recv_ref, chosen_hbm, out_ref, rows, chosen_ref, sem):
    load = pltpu.make_async_copy(chosen_hbm, chosen_ref, sem)
    load.start()
    order = row_permutation(final_source)
    for blk in range(recv_ref.shape[0] // BLOCK):
        moved = pick(order, recv_ref[blk * BLOCK : blk * BLOCK + BLOCK, :])
        for f in range(4):
            rows[blk * 64 : blk * 64 + 64, f * 128 : f * 128 + 128] = moved[f * 64 : f * 64 + 64, :]
    load.wait()
    total = lax.dot_general(
        chosen_ref[...], rows[...], CONTRACT_FIRST, preferred_element_type=F32
    )
    out_ref[...] = total.astype(BF16)


def grads_kernel(own, last_p, last_m, plain_p, plain_m, up_out, down_out):
    half = last_p.shape[0] // 2
    for w, out in enumerate((up_out, down_out)):
        one = slice(w * half, w * half + half)
        low = slice(2 * w * half, 2 * w * half + half)
        high = slice(2 * w * half + half, 2 * w * half + 2 * half)
        out[:half, :] = (
            own[low, :].astype(F32) + last_p[one, :].astype(F32) + plain_m[one, :].astype(F32)
        ).astype(BF16)
        out[half:, :] = (
            own[high, :].astype(F32) + plain_p[one, :].astype(F32) + last_m[one, :].astype(F32)
        ).astype(BF16)


def shape(dims, dtype=BF16):
    return jax.ShapeDtypeStruct(dims, dtype)


def on_chip(dims):
    return pltpu.VMEM(dims, BF16)


def in_hbm(dims):
    return pltpu.HBM(dims, BF16)


def keep(value):
    return pltpu.with_memory_space_constraint(value, pltpu.VMEM)


def leave(value):
    return pltpu.with_memory_space_constraint(value, pltpu.HBM)


PARAMS = pltpu.CompilerParams(vmem_limit_bytes=VMEM_LIMIT)


def local(inputs, out_grad, gate_weights, routes, up_weight, down_weight):
    expert_count = lax.axis_size("expert")
    dp_count = lax.axis_size("dp")
    token_count, route_count = routes.shape
    capacity = 8
    slot_rows = expert_count * capacity
    row_count = slot_rows // dp_count
    part = inputs.shape[1]
    width = part * dp_count
    peers = expert_count * dp_count
    hidden_part = up_weight.shape[1]
    hidden = hidden_part * dp_count
    half = hidden_part // 2

    def shift(value, by):
        pairs = [(i, (i + by) % dp_count) for i in range(dp_count)]
        return lax.ppermute(value, "dp", pairs)

    def swap(values):
        lanes = values.shape[1]
        moved = lax.all_to_all(
            values.reshape(peers, 8, lanes), ("expert", "dp"), split_axis=0, concat_axis=0, tiled=True
        )
        return moved.reshape(peers * 8, lanes)

    hbm = pl.BlockSpec(memory_space=pltpu.HBM)
    vmem = pl.BlockSpec(memory_space=pltpu.VMEM)
    send_rows = slot_rows * 4
    send, chosen = pl.pallas_call(
        dispatch_kernel,
        in_specs=[hbm] * 4,
        out_specs=(hbm, hbm),
        out_shape=(in_hbm((send_rows, BLOCK)), in_hbm((slot_rows, token_count))),
        scratch_shapes=[
            pltpu.VMEM((route_count, token_count), I32),
            pltpu.VMEM((route_count, token_count), F32),
            pltpu.VMEM((token_count, part), BF16),
            pltpu.VMEM((token_count, part), BF16),
            pltpu.VMEM((send_rows, BLOCK), BF16),
            pltpu.VMEM((slot_rows, token_count), BF16),
            pltpu.VMEM((slot_rows, part), BF16),
            pltpu.VMEM((slot_rows, part), BF16),
            pltpu.SemaphoreType.DMA((CHUNKS,)),
            pltpu.SemaphoreType.DMA((4,)),
            pltpu.SemaphoreType.DMA(()),
        ],
        compiler_params=PARAMS,
        name="dispatch",
    )(*[leave(value) for value in (routes.T, gate_weights.T, inputs, out_grad)])
    recv = swap(send)

    up_own, down_own = up_weight[0], down_weight[0]
    ups = [up_own] + [shift(up_own, by) for by in (-1, 1, 2)]
    downs = [down_own] + [shift(down_own, by) for by in (-1, 1, 2)]
    weights = [leave(value) for value in ups + downs]

    piece = (hidden_part, width)
    whole = (2 * hidden_part, width)
    rows_shape, hidden_shape = (row_count, width), (hidden, row_count)
    d_pre, up_full, hidden_t, d_pre_t, in_rows, grad_rows, first_p, first_m = pl.pallas_call(
        expert_kernel,
        in_specs=[vmem] + [hbm] * 8,
        out_specs=(vmem,) * 2 + (hbm,) * 6,
        out_shape=(on_chip(hidden_shape), on_chip((hidden, width)))
        + (in_hbm(hidden_shape),) * 2
        + (in_hbm(rows_shape),) * 2
        + (in_hbm(piece),) * 2,
        scratch_shapes=[pltpu.VMEM((hidden, width), BF16), pltpu.VMEM(hidden_shape, BF16)]
        + [pltpu.VMEM(rows_shape, BF16)] * 2
        + [pltpu.VMEM(piece, BF16)] * 2
        + [pltpu.SemaphoreType.DMA((8,)), pltpu.SemaphoreType.DMA((6,))],
        compiler_params=PARAMS,
        name="expert",
    )(keep(recv), *weights)

    got_p, got_m = shift(first_p, 1), shift(first_m, -1)
    ret = pl.pallas_call(
        return_kernel,
        out_specs=hbm,
        out_shape=in_hbm((send_rows, 128)),
        scratch_shapes=[pltpu.VMEM((send_rows, 128), BF16), pltpu.SemaphoreType.DMA((CHUNKS,))],
        compiler_params=PARAMS,
        name="rows_back",
    )(keep(d_pre), keep(up_full))
    returned = swap(ret)
    plain_p, plain_m, held_p, held_m, own = pl.pallas_call(
        rest_kernel,
        in_specs=[hbm] * 4,
        out_specs=(hbm,) * 5,
        out_shape=(in_hbm(piece),) * 4 + (in_hbm(whole),),
        scratch_shapes=[pltpu.VMEM(hidden_shape, BF16)] * 2
        + [pltpu.VMEM(rows_shape, BF16)] * 2
        + [pltpu.VMEM(piece, BF16)] * 4
        + [
            pltpu.VMEM(whole, BF16),
            pltpu.SemaphoreType.DMA((5,)),
            pltpu.SemaphoreType.DMA((4,)),
        ],
        compiler_params=PARAMS,
        name="rest",
    )(*[leave(value) for value in (d_pre_t, hidden_t, in_rows, grad_rows)])
    plain_p, plain_m = shift(plain_p, 1), shift(plain_m, -1)
    last_p = shift((held_p.astype(F32) + got_p.astype(F32)).astype(BF16), 1)
    last_m = shift((held_m.astype(F32) + got_m.astype(F32)).astype(BF16), -1)
    grad_up, grad_down = pl.pallas_call(
        grads_kernel,
        out_shape=(shape(piece), shape(piece)),
        compiler_params=PARAMS,
        cost_estimate=pl.CostEstimate(flops=3 * 10**10, transcendentals=0, bytes_accessed=6 * 10**6),
        name="grads",
    )(keep(own), keep(last_p), keep(last_m), keep(plain_p), keep(plain_m))

    in_grad = pl.pallas_call(
        combine_kernel,
        out_shape=shape((token_count, part)),
        in_specs=[vmem, hbm],
        scratch_shapes=[
            pltpu.VMEM((slot_rows, part), BF16),
            pltpu.VMEM((slot_rows, token_count), BF16),
            pltpu.SemaphoreType.DMA(()),
        ],
        compiler_params=PARAMS,
        name="combine",
    )(keep(returned), leave(chosen))
    return (in_grad, grad_up[None], grad_down[None])


def solution(mesh):
    return jax.shard_map(
        local,
        mesh=mesh,
        in_specs=(
            P("expert", "dp"),
            P("expert", "dp"),
            P("expert", None),
            P("expert", None),
            P("expert", "dp", None),
            P("expert", "dp", None),
        ),
        out_specs=(P("expert", "dp"), P("expert", "dp", None), P("expert", "dp", None)),
        check_vma=False,
    )
```

```python
import jax
import jax.numpy as jnp
from jax import lax
from jax.experimental import pallas as pl
from jax.experimental.pallas import tpu as pltpu
from jax.sharding import PartitionSpec as P

F32 = jnp.float32
BF16 = jnp.bfloat16
I32 = jnp.int32
CONTRACT_LAST = (((1,), (1,)), ((), ()))
CONTRACT_FIRST = (((0,), (0,)), ((), ()))
BLOCK = 256
VMEM_LIMIT = 32 * 1024 * 1024


def bits(values, low, count):
    return (values >> low) & ((1 << count) - 1)


def row_permutation(source_of):
    row = lax.broadcasted_iota(I32, (BLOCK, BLOCK), 0)
    col = lax.broadcasted_iota(I32, (BLOCK, BLOCK), 1)
    return (col == source_of(row)).astype(F32).astype(BF16)


def pick(matrix, values):
    return jnp.dot(matrix, values, preferred_element_type=F32).astype(BF16)


def send_source(i):
    e, q, h, a, r = bits(i, 5, 3), bits(i, 3, 2), bits(i, 2, 1), bits(i, 1, 1), bits(i, 0, 1)
    return a * 128 + h * 64 + e * 8 + q * 2 + r


def lanes_source(i):
    g, e, r = bits(i, 4, 4), bits(i, 1, 3), bits(i, 0, 1)
    return e * 32 + g * 2 + r


def rows_source(i):
    e, g, r = bits(i, 5, 3), bits(i, 1, 4), bits(i, 0, 1)
    return g * 16 + e * 2 + r


def final_source(i):
    f, e, q, r = bits(i, 6, 2), bits(i, 3, 3), bits(i, 1, 2), bits(i, 0, 1)
    return e * 32 + q * 8 + f * 2 + r


CHUNKS = 4


def chunk_copy(src, dst, sems, i):
    rows = src.shape[0] // CHUNKS
    at = pl.ds(i * rows, rows)
    return pltpu.make_async_copy(src.at[at, :], dst.at[at, :], sems.at[i])


def drain(src, dst, sems, blk):
    per_chunk = src.shape[0] // BLOCK // CHUNKS
    if (blk + 1) % per_chunk == 0:
        chunk_copy(src, dst, sems, blk // per_chunk).start()


def finish(src, dst, sems):
    for i in range(CHUNKS):
        chunk_copy(src, dst, sems, i).wait()


def dispatch_kernel(
    routes_hbm, gates_hbm, in_hbm_ref, out_hbm_ref, send_hbm, chosen_ref,
    routes_ref, gates_ref, in_ref, out_ref, send_ref, nat_in, nat_grad, sems, in_sems,
):
    loads = [
        pltpu.make_async_copy(src, dst, in_sems.at[i])
        for i, (src, dst) in enumerate(
            (
                (routes_hbm, routes_ref), (gates_hbm, gates_ref),
                (in_hbm_ref, in_ref), (out_hbm_ref, out_ref),
            )
        )
    ]
    for load in loads:
        load.start()
    for load in loads[:2]:
        load.wait()
    route_count, tokens = routes_ref.shape
    slot_rows = chosen_ref.shape[0]
    capacity = 8
    experts = slot_rows // capacity
    expert_id = lax.broadcasted_iota(I32, (experts, tokens), 0)
    match = jnp.zeros((experts, tokens), F32)
    gates = jnp.zeros((experts, tokens), F32)
    for k in range(route_count):
        hit = routes_ref[k : k + 1, :] == expert_id
        match = jnp.where(hit, 1.0, match)
        gates = jnp.where(hit, gates_ref[k : k + 1, :], gates)
    before = lax.broadcasted_iota(I32, (tokens, tokens), 0)
    after = lax.broadcasted_iota(I32, (tokens, tokens), 1)
    earlier = jnp.where(before < after, 1.0, 0.0).astype(BF16)
    ranks = jnp.dot(match.astype(BF16), earlier, preferred_element_type=F32)
    ranks = jnp.where(match > 0.0, ranks, -1.0)
    slot = lax.broadcasted_iota(I32, (experts, capacity, tokens), 1).astype(F32)
    chosen = jnp.where(ranks[:, None, :] == slot, 1.0, 0.0)
    slot_gates = jnp.sum((chosen * gates[:, None, :]).reshape(slot_rows, tokens), axis=1, keepdims=True)
    chosen = chosen.reshape(slot_rows, tokens).astype(BF16)
    chosen_ref[...] = chosen
    for load in loads[2:]:
        load.wait()
    nat_in[...] = jnp.dot(chosen, in_ref[...], preferred_element_type=F32).astype(BF16)
    scaled = slot_gates * jnp.dot(chosen, out_ref[...], preferred_element_type=F32)
    nat_grad[...] = scaled.astype(BF16)
    order = row_permutation(send_source)
    for blk in range(send_ref.shape[0] // BLOCK):
        at = slice(blk * 64, blk * 64 + 64)
        parts = [nat[at, h * BLOCK : h * BLOCK + BLOCK] for nat in (nat_in, nat_grad) for h in (0, 1)]
        send_ref[blk * BLOCK : blk * BLOCK + BLOCK, :] = pick(order, jnp.concatenate(parts, axis=0))
        drain(send_ref, send_hbm, sems, blk)
    finish(send_ref, send_hbm, sems)


def expert_kernel(
    recv_ref, u0, u1, u2, u3, d0, d1, d2, d3,
    ret_hbm, own_out, first_p, first_m, plain_p, plain_m, held_p, held_m,
    up, down, in_rows, grad_rows, ret_ref, own_s, fp_s, fm_s, pp_s, pm_s, hp_s, hm_s,
    sems, out_sems, ret_sems,
):
    part = u0.shape[0]
    half = part // 2
    copies = []
    for i, (ref, full) in enumerate(
        [(r, up) for r in (u0, u1, u2, u3)] + [(r, down) for r in (d0, d1, d2, d3)]
    ):
        at = (i % 4) * part
        copies.append(pltpu.make_async_copy(ref, full.at[pl.ds(at, part), :], sems.at[i]))
        copies[-1].start()
    to_lanes = row_permutation(lanes_source)
    for blk in range(recv_ref.shape[0] // BLOCK):
        moved = pick(to_lanes, recv_ref[blk * BLOCK : blk * BLOCK + BLOCK, :])
        for g in range(8):
            for a, rows in ((0, in_rows), (1, grad_rows)):
                rows[blk * 16 : blk * 16 + 16, g * BLOCK : g * BLOCK + BLOCK] = moved[
                    (2 * g + a) * 16 : (2 * g + a) * 16 + 16, :
                ]
    for copy in copies[:4]:
        copy.wait()
    pre = lax.dot_general(up[...], in_rows[...], CONTRACT_LAST, preferred_element_type=F32)
    for copy in copies[4:]:
        copy.wait()
    back = lax.dot_general(down[...], grad_rows[...], CONTRACT_LAST, preferred_element_type=F32)
    sigma = jax.nn.sigmoid(pre)
    hidden = (pre * sigma).astype(BF16)
    d_pre = (back * sigma * (1.0 + pre * (1.0 - sigma))).astype(BF16)

    outs = []

    def send(i, src, dst):
        outs.append(pltpu.make_async_copy(src, dst, out_sems.at[i]))
        outs[-1].start()

    width = in_rows.shape[1]
    step = 512
    for top in (0, part, 2 * part, 3 * part):
        for w, (left, rows) in enumerate(((d_pre, in_rows), (hidden, grad_rows))):
            one, two = slice(w * half, w * half + half), slice(w * part, w * part + part)
            for n in range(width // step):
                lanes = slice(n * step, n * step + step)
                total = jnp.dot(
                    left[top : top + part], rows[:, lanes], preferred_element_type=F32
                ).astype(BF16)
                if top == 0:
                    own_s[two, lanes] = total
                elif top == part:
                    hp_s[one, lanes] = total[:half]
                    pp_s[one, lanes] = total[half:]
                elif top == 2 * part:
                    pm_s[one, lanes] = total[:half]
                    hm_s[one, lanes] = total[half:]
                else:
                    fp_s[one, lanes] = total[:half]
                    fm_s[one, lanes] = total[half:]
        if top == 0:
            send(6, own_s, own_out)
        elif top == part:
            send(4, hp_s, held_p)
            send(2, pp_s, plain_p)
        elif top == 2 * part:
            send(3, pm_s, plain_m)
            send(5, hm_s, held_m)
        else:
            send(0, fp_s, first_p)
            send(1, fm_s, first_m)
    rows_back = lax.dot_general(d_pre, up[...], CONTRACT_FIRST, preferred_element_type=F32)
    rows_back = rows_back.astype(BF16)
    to_rows = row_permutation(rows_source)
    for blk in range(ret_ref.shape[0] // BLOCK):
        parts = [rows_back[blk * 16 : blk * 16 + 16, g * 128 : g * 128 + 128] for g in range(16)]
        ret_ref[blk * BLOCK : blk * BLOCK + BLOCK, :] = pick(to_rows, jnp.concatenate(parts, axis=0))
        drain(ret_ref, ret_hbm, ret_sems, blk)
    finish(ret_ref, ret_hbm, ret_sems)
    for copy in outs:
        copy.wait()


def combine_kernel(recv_ref, chosen_ref, out_ref, rows):
    order = row_permutation(final_source)
    for blk in range(recv_ref.shape[0] // BLOCK):
        moved = pick(order, recv_ref[blk * BLOCK : blk * BLOCK + BLOCK, :])
        for f in range(4):
            rows[blk * 64 : blk * 64 + 64, f * 128 : f * 128 + 128] = moved[f * 64 : f * 64 + 64, :]
    total = lax.dot_general(
        chosen_ref[...], rows[...], CONTRACT_FIRST, preferred_element_type=F32
    )
    out_ref[...] = total.astype(BF16)


def grads_kernel(own, last_p, last_m, plain_p, plain_m, up_out, down_out):
    half = last_p.shape[0] // 2
    for w, out in enumerate((up_out, down_out)):
        one = slice(w * half, w * half + half)
        low = slice(2 * w * half, 2 * w * half + half)
        high = slice(2 * w * half + half, 2 * w * half + 2 * half)
        out[:half, :] = (
            own[low, :].astype(F32) + last_p[one, :].astype(F32) + plain_m[one, :].astype(F32)
        ).astype(BF16)
        out[half:, :] = (
            own[high, :].astype(F32) + plain_p[one, :].astype(F32) + last_m[one, :].astype(F32)
        ).astype(BF16)


def shape(dims, dtype=BF16):
    return jax.ShapeDtypeStruct(dims, dtype)


def on_chip(dims):
    return pltpu.VMEM(dims, BF16)


def in_hbm(dims):
    return pltpu.HBM(dims, BF16)


def keep(value):
    return pltpu.with_memory_space_constraint(value, pltpu.VMEM)


def leave(value):
    return pltpu.with_memory_space_constraint(value, pltpu.HBM)


PARAMS = pltpu.CompilerParams(vmem_limit_bytes=VMEM_LIMIT)


def local(inputs, out_grad, gate_weights, routes, up_weight, down_weight):
    expert_count = lax.axis_size("expert")
    dp_count = lax.axis_size("dp")
    token_count, route_count = routes.shape
    capacity = 8
    slot_rows = expert_count * capacity
    row_count = slot_rows // dp_count
    part = inputs.shape[1]
    width = part * dp_count
    peers = expert_count * dp_count
    hidden_part = up_weight.shape[1]
    hidden = hidden_part * dp_count
    half = hidden_part // 2

    def shift(value, by):
        pairs = [(i, (i + by) % dp_count) for i in range(dp_count)]
        return lax.ppermute(value, "dp", pairs)

    def swap(values):
        lanes = values.shape[1]
        moved = lax.all_to_all(
            values.reshape(peers, 8, lanes), ("expert", "dp"), split_axis=0, concat_axis=0, tiled=True
        )
        return moved.reshape(peers * 8, lanes)

    hbm = pl.BlockSpec(memory_space=pltpu.HBM)
    vmem = pl.BlockSpec(memory_space=pltpu.VMEM)
    send_rows = slot_rows * 4
    send, chosen = pl.pallas_call(
        dispatch_kernel,
        in_specs=[hbm] * 4,
        out_specs=(hbm, vmem),
        out_shape=(in_hbm((send_rows, BLOCK)), on_chip((slot_rows, token_count))),
        scratch_shapes=[
            pltpu.VMEM((route_count, token_count), I32),
            pltpu.VMEM((route_count, token_count), F32),
            pltpu.VMEM((token_count, part), BF16),
            pltpu.VMEM((token_count, part), BF16),
            pltpu.VMEM((send_rows, BLOCK), BF16),
            pltpu.VMEM((slot_rows, part), BF16),
            pltpu.VMEM((slot_rows, part), BF16),
            pltpu.SemaphoreType.DMA((CHUNKS,)),
            pltpu.SemaphoreType.DMA((4,)),
        ],
        compiler_params=PARAMS,
        name="dispatch",
    )(*[leave(value) for value in (routes.T, gate_weights.T, inputs, out_grad)])
    recv = swap(send)

    up_own, down_own = up_weight[0], down_weight[0]
    ups = [up_own] + [shift(up_own, by) for by in (-1, 1, 2)]
    downs = [down_own] + [shift(down_own, by) for by in (-1, 1, 2)]
    weights = [leave(value) for value in ups + downs]

    piece = (hidden_part, width)
    whole = (2 * hidden_part, width)
    ret, own, first_p, first_m, plain_p, plain_m, held_p, held_m = pl.pallas_call(
        expert_kernel,
        in_specs=[vmem] + [hbm] * 8,
        out_specs=(hbm,) * 8,
        out_shape=(in_hbm((send_rows, 128)), in_hbm(whole)) + (in_hbm(piece),) * 6,
        scratch_shapes=[pltpu.VMEM((hidden, width), BF16)] * 2
        + [pltpu.VMEM((row_count, width), BF16)] * 2
        + [pltpu.VMEM((send_rows, 128), BF16), pltpu.VMEM(whole, BF16)]
        + [pltpu.VMEM(piece, BF16)] * 6
        + [pltpu.SemaphoreType.DMA((n,)) for n in (8, 7, CHUNKS)],
        compiler_params=PARAMS,
        name="expert",
    )(keep(recv), *weights)

    got_p, got_m = shift(first_p, 1), shift(first_m, -1)
    returned = swap(ret)
    plain_p, plain_m = shift(plain_p, 1), shift(plain_m, -1)
    last_p = shift((held_p.astype(F32) + got_p.astype(F32)).astype(BF16), 1)
    last_m = shift((held_m.astype(F32) + got_m.astype(F32)).astype(BF16), -1)
    grad_up, grad_down = pl.pallas_call(
        grads_kernel,
        out_shape=(shape(piece), shape(piece)),
        compiler_params=PARAMS,
        cost_estimate=pl.CostEstimate(flops=3 * 10**10, transcendentals=0, bytes_accessed=6 * 10**6),
        name="grads",
    )(keep(own), keep(last_p), keep(last_m), keep(plain_p), keep(plain_m))

    in_grad = pl.pallas_call(
        combine_kernel,
        out_shape=shape((token_count, part)),
        scratch_shapes=[pltpu.VMEM((slot_rows, part), BF16)],
        compiler_params=PARAMS,
        name="combine",
    )(keep(returned), keep(chosen))
    return (in_grad, grad_up[None], grad_down[None])


def solution(mesh):
    return jax.shard_map(
        local,
        mesh=mesh,
        in_specs=(
            P("expert", "dp"),
            P("expert", "dp"),
            P("expert", None),
            P("expert", None),
            P("expert", "dp", None),
            P("expert", "dp", None),
        ),
        out_specs=(P("expert", "dp"), P("expert", "dp", None), P("expert", "dp", None)),
        check_vma=False,
    )
```

```python
import jax
import jax.numpy as jnp
from jax import lax
from jax.experimental import pallas as pl
from jax.experimental.pallas import tpu as pltpu
from jax.sharding import PartitionSpec as P

F32 = jnp.float32
BF16 = jnp.bfloat16
I32 = jnp.int32
CONTRACT_LAST = (((1,), (1,)), ((), ()))
CONTRACT_FIRST = (((0,), (0,)), ((), ()))
BLOCK = 256
VMEM_LIMIT = 32 * 1024 * 1024


def bits(values, low, count):
    return (values >> low) & ((1 << count) - 1)


def row_permutation(source_of):
    row = lax.broadcasted_iota(I32, (BLOCK, BLOCK), 0)
    col = lax.broadcasted_iota(I32, (BLOCK, BLOCK), 1)
    return (col == source_of(row)).astype(F32).astype(BF16)


def pick(matrix, values):
    return jnp.dot(matrix, values, preferred_element_type=F32).astype(BF16)


def send_source(i):
    e, q, h, a, r = bits(i, 5, 3), bits(i, 3, 2), bits(i, 2, 1), bits(i, 1, 1), bits(i, 0, 1)
    return a * 128 + h * 64 + e * 8 + q * 2 + r


def lanes_source(i):
    g, e, r = bits(i, 4, 4), bits(i, 1, 3), bits(i, 0, 1)
    return e * 32 + g * 2 + r


def rows_source(i):
    e, g, r = bits(i, 5, 3), bits(i, 1, 4), bits(i, 0, 1)
    return g * 16 + e * 2 + r


def final_source(i):
    f, e, q, r = bits(i, 6, 2), bits(i, 3, 3), bits(i, 1, 2), bits(i, 0, 1)
    return e * 32 + q * 8 + f * 2 + r


CHUNKS = 4


def chunk_copy(src, dst, sems, i):
    rows = src.shape[0] // CHUNKS
    at = pl.ds(i * rows, rows)
    return pltpu.make_async_copy(src.at[at, :], dst.at[at, :], sems.at[i])


def drain(src, dst, sems, blk):
    per_chunk = src.shape[0] // BLOCK // CHUNKS
    if (blk + 1) % per_chunk == 0:
        chunk_copy(src, dst, sems, blk // per_chunk).start()


def finish(src, dst, sems):
    for i in range(CHUNKS):
        chunk_copy(src, dst, sems, i).wait()


def dispatch_kernel(
    routes_hbm, gates_hbm, in_hbm_ref, out_hbm_ref, send_hbm, chosen_ref,
    routes_ref, gates_ref, in_ref, out_ref, send_ref, nat_in, nat_grad, sems, in_sems,
):
    loads = [
        pltpu.make_async_copy(src, dst, in_sems.at[i])
        for i, (src, dst) in enumerate(
            (
                (routes_hbm, routes_ref), (gates_hbm, gates_ref),
                (in_hbm_ref, in_ref), (out_hbm_ref, out_ref),
            )
        )
    ]
    for load in loads:
        load.start()
    for load in loads[:2]:
        load.wait()
    route_count, tokens = routes_ref.shape
    slot_rows = chosen_ref.shape[0]
    capacity = 8
    experts = slot_rows // capacity
    expert_id = lax.broadcasted_iota(I32, (experts, tokens), 0)
    match = jnp.zeros((experts, tokens), F32)
    gates = jnp.zeros((experts, tokens), F32)
    for k in range(route_count):
        hit = routes_ref[k : k + 1, :] == expert_id
        match = jnp.where(hit, 1.0, match)
        gates = jnp.where(hit, gates_ref[k : k + 1, :], gates)
    before = lax.broadcasted_iota(I32, (tokens, tokens), 0)
    after = lax.broadcasted_iota(I32, (tokens, tokens), 1)
    earlier = jnp.where(before < after, 1.0, 0.0).astype(BF16)
    ranks = jnp.dot(match.astype(BF16), earlier, preferred_element_type=F32)
    ranks = jnp.where(match > 0.0, ranks, -1.0)
    slot = lax.broadcasted_iota(I32, (experts, capacity, tokens), 1).astype(F32)
    chosen = jnp.where(ranks[:, None, :] == slot, 1.0, 0.0)
    slot_gates = jnp.sum((chosen * gates[:, None, :]).reshape(slot_rows, tokens), axis=1, keepdims=True)
    chosen = chosen.reshape(slot_rows, tokens).astype(BF16)
    chosen_ref[...] = chosen
    for load in loads[2:]:
        load.wait()
    nat_in[...] = jnp.dot(chosen, in_ref[...], preferred_element_type=F32).astype(BF16)
    scaled = slot_gates * jnp.dot(chosen, out_ref[...], preferred_element_type=F32)
    nat_grad[...] = scaled.astype(BF16)
    order = row_permutation(send_source)
    for blk in range(send_ref.shape[0] // BLOCK):
        at = slice(blk * 64, blk * 64 + 64)
        parts = [nat[at, h * BLOCK : h * BLOCK + BLOCK] for nat in (nat_in, nat_grad) for h in (0, 1)]
        send_ref[blk * BLOCK : blk * BLOCK + BLOCK, :] = pick(order, jnp.concatenate(parts, axis=0))
        drain(send_ref, send_hbm, sems, blk)
    finish(send_ref, send_hbm, sems)


def expert_kernel(
    recv_ref, u0, u1, u2, u3, d0, d1, d2, d3,
    ret_hbm, own_out, first_p, first_m, plain_p, plain_m, held_p, held_m,
    up, down, in_rows, grad_rows, ret_ref, own_s, fp_s, fm_s, pp_s, pm_s, hp_s, hm_s,
    sems, out_sems, ret_sems,
):
    part = u0.shape[0]
    cut = first_p.shape[0] // 2
    copies = []
    for i, (ref, full) in enumerate(
        [(r, up) for r in (u0, u1, u2, u3)] + [(r, down) for r in (d0, d1, d2, d3)]
    ):
        at = (i % 4) * part
        copies.append(pltpu.make_async_copy(ref, full.at[pl.ds(at, part), :], sems.at[i]))
        copies[-1].start()
    to_lanes = row_permutation(lanes_source)
    for blk in range(recv_ref.shape[0] // BLOCK):
        moved = pick(to_lanes, recv_ref[blk * BLOCK : blk * BLOCK + BLOCK, :])
        for g in range(8):
            for a, rows in ((0, in_rows), (1, grad_rows)):
                rows[blk * 16 : blk * 16 + 16, g * BLOCK : g * BLOCK + BLOCK] = moved[
                    (2 * g + a) * 16 : (2 * g + a) * 16 + 16, :
                ]
    for copy in copies[:4]:
        copy.wait()
    pre = lax.dot_general(up[...], in_rows[...], CONTRACT_LAST, preferred_element_type=F32)
    for copy in copies[4:]:
        copy.wait()
    back = lax.dot_general(down[...], grad_rows[...], CONTRACT_LAST, preferred_element_type=F32)
    sigma = jax.nn.sigmoid(pre)
    hidden = (pre * sigma).astype(BF16)
    d_pre = (back * sigma * (1.0 + pre * (1.0 - sigma))).astype(BF16)

    outs = []

    def send(i, src, dst):
        outs.append(pltpu.make_async_copy(src, dst, out_sems.at[i]))
        outs[-1].start()

    width = in_rows.shape[1]
    step = 512
    for top in (0, part, 2 * part, 3 * part):
        for w, (left, rows) in enumerate(((d_pre, in_rows), (hidden, grad_rows))):
            low = slice(w * cut, w * cut + cut)
            high = slice(w * (part - cut), w * (part - cut) + part - cut)
            two = slice(w * part, w * part + part)
            for n in range(width // step):
                lanes = slice(n * step, n * step + step)
                total = jnp.dot(
                    left[top : top + part], rows[:, lanes], preferred_element_type=F32
                ).astype(BF16)
                if top == 0:
                    own_s[two, lanes] = total
                elif top == part:
                    hp_s[low, lanes] = total[:cut]
                    pp_s[high, lanes] = total[cut:]
                elif top == 2 * part:
                    pm_s[low, lanes] = total[:cut]
                    hm_s[high, lanes] = total[cut:]
                else:
                    fp_s[low, lanes] = total[:cut]
                    fm_s[high, lanes] = total[cut:]
        if top == 0:
            send(6, own_s, own_out)
        elif top == part:
            send(4, hp_s, held_p)
            send(2, pp_s, plain_p)
        elif top == 2 * part:
            send(3, pm_s, plain_m)
            send(5, hm_s, held_m)
        else:
            send(0, fp_s, first_p)
            send(1, fm_s, first_m)
    rows_back = lax.dot_general(d_pre, up[...], CONTRACT_FIRST, preferred_element_type=F32)
    rows_back = rows_back.astype(BF16)
    to_rows = row_permutation(rows_source)
    for blk in range(ret_ref.shape[0] // BLOCK):
        parts = [rows_back[blk * 16 : blk * 16 + 16, g * 128 : g * 128 + 128] for g in range(16)]
        ret_ref[blk * BLOCK : blk * BLOCK + BLOCK, :] = pick(to_rows, jnp.concatenate(parts, axis=0))
        drain(ret_ref, ret_hbm, ret_sems, blk)
    finish(ret_ref, ret_hbm, ret_sems)
    for copy in outs:
        copy.wait()


def combine_kernel(recv_ref, chosen_ref, out_ref, rows):
    order = row_permutation(final_source)
    for blk in range(recv_ref.shape[0] // BLOCK):
        moved = pick(order, recv_ref[blk * BLOCK : blk * BLOCK + BLOCK, :])
        for f in range(4):
            rows[blk * 64 : blk * 64 + 64, f * 128 : f * 128 + 128] = moved[f * 64 : f * 64 + 64, :]
    total = lax.dot_general(
        chosen_ref[...], rows[...], CONTRACT_FIRST, preferred_element_type=F32
    )
    out_ref[...] = total.astype(BF16)


def grads_kernel(own, last_p, last_m, plain_p, plain_m, up_out, down_out):
    part = up_out.shape[0]
    cut = last_p.shape[0] // 2
    for w, out in enumerate((up_out, down_out)):
        top = w * part
        low = slice(w * cut, w * cut + cut)
        high = slice(w * (part - cut), w * (part - cut) + part - cut)
        out[:cut, :] = (
            own[top : top + cut, :].astype(F32)
            + last_p[low, :].astype(F32)
            + plain_m[low, :].astype(F32)
        ).astype(BF16)
        out[cut:, :] = (
            own[top + cut : top + part, :].astype(F32)
            + plain_p[high, :].astype(F32)
            + last_m[high, :].astype(F32)
        ).astype(BF16)


def shape(dims, dtype=BF16):
    return jax.ShapeDtypeStruct(dims, dtype)


def on_chip(dims):
    return pltpu.VMEM(dims, BF16)


def in_hbm(dims):
    return pltpu.HBM(dims, BF16)


def keep(value):
    return pltpu.with_memory_space_constraint(value, pltpu.VMEM)


def leave(value):
    return pltpu.with_memory_space_constraint(value, pltpu.HBM)


PARAMS = pltpu.CompilerParams(vmem_limit_bytes=VMEM_LIMIT)


def local(inputs, out_grad, gate_weights, routes, up_weight, down_weight):
    expert_count = lax.axis_size("expert")
    dp_count = lax.axis_size("dp")
    token_count, route_count = routes.shape
    capacity = 8
    slot_rows = expert_count * capacity
    row_count = slot_rows // dp_count
    part = inputs.shape[1]
    width = part * dp_count
    peers = expert_count * dp_count
    hidden_part = up_weight.shape[1]
    hidden = hidden_part * dp_count
    cut = hidden_part * 3 // 4

    def shift(value, by):
        pairs = [(i, (i + by) % dp_count) for i in range(dp_count)]
        return lax.ppermute(value, "dp", pairs)

    def swap(values):
        lanes = values.shape[1]
        moved = lax.all_to_all(
            values.reshape(peers, 8, lanes), ("expert", "dp"), split_axis=0, concat_axis=0, tiled=True
        )
        return moved.reshape(peers * 8, lanes)

    hbm = pl.BlockSpec(memory_space=pltpu.HBM)
    vmem = pl.BlockSpec(memory_space=pltpu.VMEM)
    send_rows = slot_rows * 4
    send, chosen = pl.pallas_call(
        dispatch_kernel,
        in_specs=[hbm] * 4,
        out_specs=(hbm, vmem),
        out_shape=(in_hbm((send_rows, BLOCK)), on_chip((slot_rows, token_count))),
        scratch_shapes=[
            pltpu.VMEM((route_count, token_count), I32),
            pltpu.VMEM((route_count, token_count), F32),
            pltpu.VMEM((token_count, part), BF16),
            pltpu.VMEM((token_count, part), BF16),
            pltpu.VMEM((send_rows, BLOCK), BF16),
            pltpu.VMEM((slot_rows, part), BF16),
            pltpu.VMEM((slot_rows, part), BF16),
            pltpu.SemaphoreType.DMA((CHUNKS,)),
            pltpu.SemaphoreType.DMA((4,)),
        ],
        compiler_params=PARAMS,
        name="dispatch",
    )(*[leave(value) for value in (routes.T, gate_weights.T, inputs, out_grad)])
    recv = swap(send)

    up_own, down_own = up_weight[0], down_weight[0]
    ups = [up_own] + [shift(up_own, by) for by in (-1, 1, 2)]
    downs = [down_own] + [shift(down_own, by) for by in (-1, 1, 2)]
    weights = [leave(value) for value in ups + downs]

    piece = (hidden_part, width)
    lows, highs = (2 * cut, width), (2 * (hidden_part - cut), width)
    pieces = (lows, highs, highs, lows, lows, highs)
    whole = (2 * hidden_part, width)
    ret, own, first_p, first_m, plain_p, plain_m, held_p, held_m = pl.pallas_call(
        expert_kernel,
        in_specs=[vmem] + [hbm] * 8,
        out_specs=(hbm,) * 8,
        out_shape=(in_hbm((send_rows, 128)), in_hbm(whole)) + tuple(in_hbm(dims) for dims in pieces),
        scratch_shapes=[pltpu.VMEM((hidden, width), BF16)] * 2
        + [pltpu.VMEM((row_count, width), BF16)] * 2
        + [pltpu.VMEM((send_rows, 128), BF16), pltpu.VMEM(whole, BF16)]
        + [pltpu.VMEM(dims, BF16) for dims in pieces]
        + [pltpu.SemaphoreType.DMA((n,)) for n in (8, 7, CHUNKS)],
        compiler_params=PARAMS,
        name="expert",
    )(keep(recv), *weights)

    got_p, got_m = shift(first_p, 1), shift(first_m, -1)
    returned = swap(ret)
    plain_p, plain_m = shift(plain_p, 1), shift(plain_m, -1)
    last_p = shift((held_p.astype(F32) + got_p.astype(F32)).astype(BF16), 1)
    last_m = shift((held_m.astype(F32) + got_m.astype(F32)).astype(BF16), -1)
    grad_up, grad_down = pl.pallas_call(
        grads_kernel,
        out_shape=(shape(piece), shape(piece)),
        compiler_params=PARAMS,
        cost_estimate=pl.CostEstimate(flops=3 * 10**10, transcendentals=0, bytes_accessed=6 * 10**6),
        name="grads",
    )(keep(own), keep(last_p), keep(last_m), keep(plain_p), keep(plain_m))

    in_grad = pl.pallas_call(
        combine_kernel,
        out_shape=shape((token_count, part)),
        scratch_shapes=[pltpu.VMEM((slot_rows, part), BF16)],
        compiler_params=PARAMS,
        name="combine",
    )(keep(returned), keep(chosen))
    return (in_grad, grad_up[None], grad_down[None])


def solution(mesh):
    return jax.shard_map(
        local,
        mesh=mesh,
        in_specs=(
            P("expert", "dp"),
            P("expert", "dp"),
            P("expert", None),
            P("expert", None),
            P("expert", "dp", None),
            P("expert", "dp", None),
        ),
        out_specs=(P("expert", "dp"), P("expert", "dp", None), P("expert", "dp", None)),
        check_vma=False,
    )
```

```python
import jax
import jax.numpy as jnp
from jax import lax
from jax.experimental import pallas as pl
from jax.experimental.pallas import tpu as pltpu
from jax.sharding import PartitionSpec as P

F32 = jnp.float32
BF16 = jnp.bfloat16
I32 = jnp.int32
CONTRACT_LAST = (((1,), (1,)), ((), ()))
CONTRACT_FIRST = (((0,), (0,)), ((), ()))
BLOCK = 256
VMEM_LIMIT = 32 * 1024 * 1024


def bits(values, low, count):
    return (values >> low) & ((1 << count) - 1)


def row_permutation(source_of):
    row = lax.broadcasted_iota(I32, (BLOCK, BLOCK), 0)
    col = lax.broadcasted_iota(I32, (BLOCK, BLOCK), 1)
    return (col == source_of(row)).astype(F32).astype(BF16)


def pick(matrix, values):
    return jnp.dot(matrix, values, preferred_element_type=F32).astype(BF16)


def send_source(i):
    e, q, h, a, r = bits(i, 5, 3), bits(i, 3, 2), bits(i, 2, 1), bits(i, 1, 1), bits(i, 0, 1)
    return a * 128 + h * 64 + e * 8 + q * 2 + r


def lanes_source(i):
    g, e, r = bits(i, 4, 4), bits(i, 1, 3), bits(i, 0, 1)
    return e * 32 + g * 2 + r


def rows_source(i):
    e, g, r = bits(i, 5, 3), bits(i, 1, 4), bits(i, 0, 1)
    return g * 16 + e * 2 + r


def final_source(i):
    f, e, q, r = bits(i, 6, 2), bits(i, 3, 3), bits(i, 1, 2), bits(i, 0, 1)
    return e * 32 + q * 8 + f * 2 + r


CHUNKS = 4


def chunk_copy(src, dst, sems, i):
    rows = src.shape[0] // CHUNKS
    at = pl.ds(i * rows, rows)
    return pltpu.make_async_copy(src.at[at, :], dst.at[at, :], sems.at[i])


def drain(src, dst, sems, blk):
    per_chunk = src.shape[0] // BLOCK // CHUNKS
    if (blk + 1) % per_chunk == 0:
        chunk_copy(src, dst, sems, blk // per_chunk).start()


def finish(src, dst, sems):
    for i in range(CHUNKS):
        chunk_copy(src, dst, sems, i).wait()


def dispatch_kernel(
    routes_hbm, gates_hbm, in_hbm_ref, out_hbm_ref, send_hbm, chosen_ref,
    routes_ref, gates_ref, in_ref, out_ref, send_ref, nat_in, nat_grad, sems, in_sems,
):
    loads = [
        pltpu.make_async_copy(src, dst, in_sems.at[i])
        for i, (src, dst) in enumerate(
            (
                (routes_hbm, routes_ref), (gates_hbm, gates_ref),
                (in_hbm_ref, in_ref), (out_hbm_ref, out_ref),
            )
        )
    ]
    for load in loads:
        load.start()
    for load in loads[:2]:
        load.wait()
    route_count, tokens = routes_ref.shape
    slot_rows = chosen_ref.shape[0]
    capacity = 8
    experts = slot_rows // capacity
    expert_id = lax.broadcasted_iota(I32, (experts, tokens), 0)
    match = jnp.zeros((experts, tokens), F32)
    gates = jnp.zeros((experts, tokens), F32)
    for k in range(route_count):
        hit = routes_ref[k : k + 1, :] == expert_id
        match = jnp.where(hit, 1.0, match)
        gates = jnp.where(hit, gates_ref[k : k + 1, :], gates)
    before = lax.broadcasted_iota(I32, (tokens, tokens), 0)
    after = lax.broadcasted_iota(I32, (tokens, tokens), 1)
    earlier = jnp.where(before < after, 1.0, 0.0).astype(BF16)
    ranks = jnp.dot(match.astype(BF16), earlier, preferred_element_type=F32)
    ranks = jnp.where(match > 0.0, ranks, -1.0)
    slot = lax.broadcasted_iota(I32, (experts, capacity, tokens), 1).astype(F32)
    chosen = jnp.where(ranks[:, None, :] == slot, 1.0, 0.0)
    slot_gates = jnp.sum((chosen * gates[:, None, :]).reshape(slot_rows, tokens), axis=1, keepdims=True)
    chosen = chosen.reshape(slot_rows, tokens).astype(BF16)
    chosen_ref[...] = chosen
    for load in loads[2:]:
        load.wait()
    nat_in[...] = jnp.dot(chosen, in_ref[...], preferred_element_type=F32).astype(BF16)
    scaled = slot_gates * jnp.dot(chosen, out_ref[...], preferred_element_type=F32)
    nat_grad[...] = scaled.astype(BF16)
    order = row_permutation(send_source)
    for blk in range(send_ref.shape[0] // BLOCK):
        at = slice(blk * 64, blk * 64 + 64)
        parts = [nat[at, h * BLOCK : h * BLOCK + BLOCK] for nat in (nat_in, nat_grad) for h in (0, 1)]
        send_ref[blk * BLOCK : blk * BLOCK + BLOCK, :] = pick(order, jnp.concatenate(parts, axis=0))
        drain(send_ref, send_hbm, sems, blk)
    finish(send_ref, send_hbm, sems)


def expert_kernel(
    recv_ref, u0, u1, u2, u3, d0, d1, d2, d3,
    ret_hbm, own_out, first_p, first_m, plain_p, plain_m, held_p, held_m,
    up, down, in_rows, grad_rows, ret_ref, own_s, fp_s, fm_s, pp_s, pm_s, hp_s, hm_s,
    sems, out_sems, ret_sems,
):
    part = u0.shape[0]
    cut = first_p.shape[0] // 2
    copies = []
    for i, (ref, full) in enumerate(
        [(r, up) for r in (u0, u1, u2, u3)] + [(r, down) for r in (d0, d1, d2, d3)]
    ):
        at = (i % 4) * part
        copies.append(pltpu.make_async_copy(ref, full.at[pl.ds(at, part), :], sems.at[i]))
        copies[-1].start()
    to_lanes = row_permutation(lanes_source)
    for blk in range(recv_ref.shape[0] // BLOCK):
        moved = pick(to_lanes, recv_ref[blk * BLOCK : blk * BLOCK + BLOCK, :])
        for g in range(8):
            for a, rows in ((0, in_rows), (1, grad_rows)):
                rows[blk * 16 : blk * 16 + 16, g * BLOCK : g * BLOCK + BLOCK] = moved[
                    (2 * g + a) * 16 : (2 * g + a) * 16 + 16, :
                ]
    for copy in copies[:4]:
        copy.wait()
    pre = lax.dot_general(up[...], in_rows[...], CONTRACT_LAST, preferred_element_type=F32)
    for copy in copies[4:]:
        copy.wait()
    back = lax.dot_general(down[...], grad_rows[...], CONTRACT_LAST, preferred_element_type=F32)
    sigma = jax.nn.sigmoid(pre)
    hidden = (pre * sigma).astype(BF16)
    d_pre = (back * sigma * (1.0 + pre * (1.0 - sigma))).astype(BF16)

    outs = []

    def send(i, src, dst):
        outs.append(pltpu.make_async_copy(src, dst, out_sems.at[i]))
        outs[-1].start()

    width = in_rows.shape[1]
    step = 512
    for top in (0, part, 2 * part, 3 * part):
        for w, (left, rows) in enumerate(((d_pre, in_rows), (hidden, grad_rows))):
            low = slice(w * cut, w * cut + cut)
            high = slice(w * (part - cut), w * (part - cut) + part - cut)
            two = slice(w * part, w * part + part)
            for n in range(width // step):
                lanes = slice(n * step, n * step + step)
                total = jnp.dot(
                    left[top : top + part], rows[:, lanes], preferred_element_type=F32
                ).astype(BF16)
                if top == 0:
                    own_s[two, lanes] = total
                elif top == part:
                    hp_s[low, lanes] = total[:cut]
                    pp_s[high, lanes] = total[cut:]
                elif top == 2 * part:
                    pm_s[low, lanes] = total[:cut]
                    hm_s[high, lanes] = total[cut:]
                else:
                    fp_s[low, lanes] = total[:cut]
                    fm_s[high, lanes] = total[cut:]
        if top == 0:
            send(6, own_s, own_out)
        elif top == part:
            send(4, hp_s, held_p)
            send(2, pp_s, plain_p)
        elif top == 2 * part:
            send(3, pm_s, plain_m)
            send(5, hm_s, held_m)
        else:
            send(0, fp_s, first_p)
            send(1, fm_s, first_m)
    rows_back = lax.dot_general(d_pre, up[...], CONTRACT_FIRST, preferred_element_type=F32)
    rows_back = rows_back.astype(BF16)
    to_rows = row_permutation(rows_source)
    for blk in range(ret_ref.shape[0] // BLOCK):
        parts = [rows_back[blk * 16 : blk * 16 + 16, g * 128 : g * 128 + 128] for g in range(16)]
        ret_ref[blk * BLOCK : blk * BLOCK + BLOCK, :] = pick(to_rows, jnp.concatenate(parts, axis=0))
        drain(ret_ref, ret_hbm, ret_sems, blk)
    finish(ret_ref, ret_hbm, ret_sems)
    for copy in outs:
        copy.wait()


def combine_kernel(recv_ref, chosen_ref, out_ref, rows):
    order = row_permutation(final_source)
    for blk in range(recv_ref.shape[0] // BLOCK):
        moved = pick(order, recv_ref[blk * BLOCK : blk * BLOCK + BLOCK, :])
        for f in range(4):
            rows[blk * 64 : blk * 64 + 64, f * 128 : f * 128 + 128] = moved[f * 64 : f * 64 + 64, :]
    total = lax.dot_general(
        chosen_ref[...], rows[...], CONTRACT_FIRST, preferred_element_type=F32
    )
    out_ref[...] = total.astype(BF16)


def grads_kernel(own, last_p, last_m, plain_p, plain_m, up_out, down_out):
    part = up_out.shape[0]
    cut = last_p.shape[0] // 2
    for w, out in enumerate((up_out, down_out)):
        top = w * part
        low = slice(w * cut, w * cut + cut)
        high = slice(w * (part - cut), w * (part - cut) + part - cut)
        out[:cut, :] = (
            own[top : top + cut, :].astype(F32)
            + last_p[low, :].astype(F32)
            + plain_m[low, :].astype(F32)
        ).astype(BF16)
        out[cut:, :] = (
            own[top + cut : top + part, :].astype(F32)
            + plain_p[high, :].astype(F32)
            + last_m[high, :].astype(F32)
        ).astype(BF16)


def shape(dims, dtype=BF16):
    return jax.ShapeDtypeStruct(dims, dtype)


def on_chip(dims):
    return pltpu.VMEM(dims, BF16)


def in_hbm(dims):
    return pltpu.HBM(dims, BF16)


def keep(value):
    return pltpu.with_memory_space_constraint(value, pltpu.VMEM)


def leave(value):
    return pltpu.with_memory_space_constraint(value, pltpu.HBM)


PARAMS = pltpu.CompilerParams(vmem_limit_bytes=VMEM_LIMIT)


def local(inputs, out_grad, gate_weights, routes, up_weight, down_weight):
    expert_count = lax.axis_size("expert")
    dp_count = lax.axis_size("dp")
    token_count, route_count = routes.shape
    capacity = 8
    slot_rows = expert_count * capacity
    row_count = slot_rows // dp_count
    part = inputs.shape[1]
    width = part * dp_count
    peers = expert_count * dp_count
    hidden_part = up_weight.shape[1]
    hidden = hidden_part * dp_count
    cut = hidden_part * 5 // 6

    def shift(value, by):
        pairs = [(i, (i + by) % dp_count) for i in range(dp_count)]
        return lax.ppermute(value, "dp", pairs)

    def swap(values):
        lanes = values.shape[1]
        moved = lax.all_to_all(
            values.reshape(peers, 8, lanes), ("expert", "dp"), split_axis=0, concat_axis=0, tiled=True
        )
        return moved.reshape(peers * 8, lanes)

    hbm = pl.BlockSpec(memory_space=pltpu.HBM)
    vmem = pl.BlockSpec(memory_space=pltpu.VMEM)
    send_rows = slot_rows * 4
    send, chosen = pl.pallas_call(
        dispatch_kernel,
        in_specs=[hbm] * 4,
        out_specs=(hbm, vmem),
        out_shape=(in_hbm((send_rows, BLOCK)), on_chip((slot_rows, token_count))),
        scratch_shapes=[
            pltpu.VMEM((route_count, token_count), I32),
            pltpu.VMEM((route_count, token_count), F32),
            pltpu.VMEM((token_count, part), BF16),
            pltpu.VMEM((token_count, part), BF16),
            pltpu.VMEM((send_rows, BLOCK), BF16),
            pltpu.VMEM((slot_rows, part), BF16),
            pltpu.VMEM((slot_rows, part), BF16),
            pltpu.SemaphoreType.DMA((CHUNKS,)),
            pltpu.SemaphoreType.DMA((4,)),
        ],
        compiler_params=PARAMS,
        name="dispatch",
    )(*[leave(value) for value in (routes.T, gate_weights.T, inputs, out_grad)])
    recv = swap(send)

    up_own, down_own = up_weight[0], down_weight[0]
    ups = [up_own] + [shift(up_own, by) for by in (1, -1, 2)]
    downs = [down_own] + [shift(down_own, by) for by in (1, -1, 2)]
    weights = [leave(value) for value in ups + downs]

    piece = (hidden_part, width)
    lows, highs = (2 * cut, width), (2 * (hidden_part - cut), width)
    pieces = (lows, highs, highs, lows, lows, highs)
    whole = (2 * hidden_part, width)
    ret, own, first_p, first_m, plain_p, plain_m, held_p, held_m = pl.pallas_call(
        expert_kernel,
        in_specs=[vmem] + [hbm] * 8,
        out_specs=(hbm,) * 8,
        out_shape=(in_hbm((send_rows, 128)), in_hbm(whole)) + tuple(in_hbm(dims) for dims in pieces),
        scratch_shapes=[pltpu.VMEM((hidden, width), BF16)] * 2
        + [pltpu.VMEM((row_count, width), BF16)] * 2
        + [pltpu.VMEM((send_rows, 128), BF16), pltpu.VMEM(whole, BF16)]
        + [pltpu.VMEM(dims, BF16) for dims in pieces]
        + [pltpu.SemaphoreType.DMA((n,)) for n in (8, 7, CHUNKS)],
        compiler_params=PARAMS,
        name="expert",
    )(keep(recv), *weights)

    got_p, got_m = shift(first_p, -1), shift(first_m, 1)
    returned = swap(ret)
    plain_p, plain_m = shift(plain_p, -1), shift(plain_m, 1)
    last_p = shift((held_p.astype(F32) + got_p.astype(F32)).astype(BF16), -1)
    last_m = shift((held_m.astype(F32) + got_m.astype(F32)).astype(BF16), 1)
    grad_up, grad_down = pl.pallas_call(
        grads_kernel,
        out_shape=(shape(piece), shape(piece)),
        compiler_params=PARAMS,
        cost_estimate=pl.CostEstimate(flops=3 * 10**10, transcendentals=0, bytes_accessed=6 * 10**6),
        name="grads",
    )(keep(own), keep(last_p), keep(last_m), keep(plain_p), keep(plain_m))

    in_grad = pl.pallas_call(
        combine_kernel,
        out_shape=shape((token_count, part)),
        scratch_shapes=[pltpu.VMEM((slot_rows, part), BF16)],
        compiler_params=PARAMS,
        name="combine",
    )(keep(returned), keep(chosen))
    return (in_grad, grad_up[None], grad_down[None])


def solution(mesh):
    return jax.shard_map(
        local,
        mesh=mesh,
        in_specs=(
            P("expert", "dp"),
            P("expert", "dp"),
            P("expert", None),
            P("expert", None),
            P("expert", "dp", None),
            P("expert", "dp", None),
        ),
        out_specs=(P("expert", "dp"), P("expert", "dp", None), P("expert", "dp", None)),
        check_vma=False,
    )
```
